128 devices in a mesh: gx: 32 (over z_hi, y, x), gy: 4 (over z_lo, core).
Axes of the slice: x: 4, y: 4, z: 4 (z_hi: 2, z_lo: 2; z = z_hi * 2 + z_lo), core: 2. Of those that a mesh axis runs over, the one named last changes fastest.
Arguments:
- potential: float32 [1024, 128, 256], P('gx', 'gy'), may hold values from 0 to 1
- recovery: float32 [1024, 128, 256], P('gx', 'gy'), may hold values from 0 to 1
- fiber: float32 [2, 1024, 128, 256], P(None, 'gx', 'gy'), may hold values from -3.140625 to 3.140625
- sig_long: float32 [256], P(('gx', 'gy')), may hold values from 0.5 to 2
- sig_trans: float32 [256], P(('gx', 'gy')), may hold values from 0.1 to 0.5
- tile_region: int32 [32, 4, 8], P('gx', 'gy'), may hold values from 0 to 255
- tile_tissue: int32 [32, 4, 8], P('gx', 'gy'), may hold values from 0 to 1, as said below
- cot_potential: float32 [1024, 128, 256], P('gx', 'gy'), may hold values from -6 to 6
- cot_recovery: float32 [1024, 128, 256], P('gx', 'gy'), may hold values from -6 to 6
Outputs:
- final_potential: float32 [1024, 128, 256], P('gx', 'gy')
- adjoint_potential: float32 [1024, 128, 256], P('gx', 'gy')
- grad_long: float32 [256], P(('gx', 'gy'))
- grad_trans: float32 [256], P(('gx', 'gy'))
The draws below stay inside these ranges and needn't reach their ends.
Inputs may be any that keep to these rules, and one draw needn't show every extreme that they name: `tile_tissue`: tissue flag of each tile; at some tile indices along x (walls, never the last index) every tile, across all of y and z, is myocardium; elsewhere myocardium is sparse.
All inputs are finite; a program needn't handle non-finite values.
Results may differ from the reference program's by a relative error of at most 0.000023.
Values sent between devices are 32-bit elements; how exact they have to be, the bound alone decides.
A program may use at most 192 MiB of HBM per device.

```python
import math
import jax
import jax.numpy as jnp

TILE = 32
NZ = 256
STEPS = 4
REGIONS = 256
NX = 1024
NY = 128
TX = 32
TY = 4
TZ = 8


def draw_tile_tissue(key, part):
    wall_key = jax.random.fold_in(key, 11)
    sparse_key = jax.random.fold_in(key, 23)
    column = jnp.arange(TX, dtype=jnp.int32)[:, None, None]
    wall_draw = jax.random.randint(wall_key, (TX, 1, 1), 0, 4)
    walls = ((wall_draw == 0) | (column == 0)) & (column != TX - 1)
    sparse = (jax.random.randint(sparse_key, (TX, TY, TZ), 0, 6) == 0).astype(jnp.int32)
    tissue = jnp.where(walls, jnp.ones((TX, TY, TZ), jnp.int32), sparse)
    row = jnp.arange(TY, dtype=jnp.int32)[None, :, None]
    depth = jnp.arange(TZ, dtype=jnp.int32)[None, None, :]
    corner = (column == TX - 1) & (row == TY - 1) & (depth == TZ - 1)
    return jnp.where(corner, jnp.zeros((TX, TY, TZ), jnp.int32), tissue).astype(jnp.int32)


def touch_ends(array, stream_key, smallest, top_value):
    index_at = [jax.random.randint(jax.random.fold_in(stream_key, axis), (), 0, length) for axis, length in enumerate(array.shape)]
    widest = array.shape.index(max(array.shape))
    neighbour = index_at[:widest] + [(index_at[widest] + 1) % array.shape[widest]] + index_at[widest + 1:]
    return array.at[tuple(index_at)].set(smallest).at[tuple(neighbour)].set(top_value)


def levels(key, shape, pieces, least, high):
    loudness = 1.0
    for axis_at, blocks in pieces:
        steps = jax.random.uniform(jax.random.fold_in(jax.random.fold_in(key, 6), axis_at), (blocks,), jnp.float32, least / len(pieces), high / len(pieces))
        loudness = loudness * jnp.repeat(jnp.exp(steps), shape[axis_at] // blocks).reshape((-1,) + (1,) * (len(shape) - 1 - axis_at))
    return loudness


def scatter_about(own_key, extent, deviation, reach, split=(), held_as=jnp.bfloat16):
    array = jax.random.normal(own_key, extent, jnp.float32) * deviation
    if len(split) > 0:
        array = levels(own_key, extent, split, -0.22, 0.18) * array
    return jnp.clip(array, min=-reach, max=reach).astype(held_as)


def setup_inputs(seed: int = 0) -> dict:
    key_of = jax.random.split(jax.random.key(seed), 10)
    potential = jnp.clip(1.0 * jax.random.uniform(key_of[0], (NX, NY, NZ), jnp.float32) ** levels(key_of[0], (NX, NY, NZ), ((0, 32), (1, 4)), -0.2, 0.2), 0.0, 1.0)
    recovery = jnp.clip(1.0 * jax.random.uniform(key_of[1], (NX, NY, NZ), jnp.float32) ** levels(key_of[1], (NX, NY, NZ), ((0, 32), (1, 4)), -0.2, 0.2), 0.0, 1.0)
    fiber = jnp.clip(jax.random.uniform(key_of[2], (2, NX, NY, NZ), jnp.float32, -3.140625, 3.140625), -3.140625, 3.140625)
    sig_long = jnp.clip(jnp.exp(math.log(2.0) - 1.3862944 * jax.random.uniform(key_of[3], (REGIONS,), jnp.float32) ** levels(key_of[3], (REGIONS,), ((0, 128),), -0.2, 0.2)), 0.5, 2.0)
    sig_trans = jnp.clip(jnp.exp(math.log(0.5) - 1.609438 * jax.random.uniform(key_of[4], (REGIONS,), jnp.float32) ** levels(key_of[4], (REGIONS,), ((0, 128),), -0.2, 0.2)), 0.1, 0.5)
    tile_region = touch_ends(jax.random.randint(key_of[5], (TX, TY, TZ), 0, REGIONS), jax.random.fold_in(key_of[5], 1), 0, REGIONS - 1).astype(jnp.int32)
    tile_tissue = draw_tile_tissue(jax.random.fold_in(key_of[9], 71), 0)
    cot_potential = scatter_about(key_of[7], (NX, NY, NZ), 1.0, 6.0, ((0, 32), (1, 4)), jnp.float32)
    cot_recovery = scatter_about(key_of[8], (NX, NY, NZ), 1.0, 6.0, ((0, 32), (1, 4)), jnp.float32)
    return {"potential": potential, "recovery": recovery, "fiber": fiber, "sig_long": sig_long, "sig_trans": sig_trans, "tile_region": tile_region, "tile_tissue": tile_tissue, "cot_potential": cot_potential, "cot_recovery": cot_recovery}


UNITS = ((1, 0, 0), (0, 1, 0), (0, 0, 1))
PAIRS = ((0, 1, 3), (0, 2, 4), (1, 2, 5))
TIME_STEP = 0.05
KAPPA = 8.0
ALPHA = 0.15
EPS_W = 0.1


def shifted(padded, shift):
    sizes = padded.shape[-3:]
    return padded[..., 1 + shift[0]:sizes[0] - 1 + shift[0], 1 + shift[1]:sizes[1] - 1 + shift[1], 1 + shift[2]:sizes[2] - 1 + shift[2]]


def negate(shift):
    return tuple(-part for part in shift)


def combine_shift(left, right, sign):
    return tuple(first + sign * second for first, second in zip(left, right))


def central(padded, shift):
    return 0.5 * (shifted(padded, shift) - shifted(padded, negate(shift)))


def fiber_parts(theta, phi):
    fib = (jnp.cos(phi) * jnp.cos(theta), jnp.cos(phi) * jnp.sin(theta), jnp.sin(phi))
    squares = [fib[0] * fib[0], fib[1] * fib[1], fib[2] * fib[2]]
    crosses = [fib[0] * fib[1], fib[0] * fib[2], fib[1] * fib[2]]
    return squares, crosses


def tensor_of(theta, phi, slong, strans):
    squares, crosses = fiber_parts(theta, phi)
    excess = slong - strans
    parts = [strans + excess * value for value in squares] + [excess * value for value in crosses]
    return jnp.stack(parts)


def diffuse(field_pad, tensor_pad):
    centre = shifted(field_pad, (0, 0, 0))
    total = jnp.zeros_like(centre)
    for slot in range(3):
        unit = UNITS[slot]
        back = negate(unit)
        coeff = tensor_pad[slot]
        middle = shifted(coeff, (0, 0, 0))
        upper = 0.5 * (middle + shifted(coeff, unit))
        lower = 0.5 * (middle + shifted(coeff, back))
        total = total + upper * (shifted(field_pad, unit) - centre) - lower * (centre - shifted(field_pad, back))
    for first, second, slot in PAIRS:
        coeff = tensor_pad[slot]
        for along, across in ((UNITS[first], UNITS[second]), (UNITS[second], UNITS[first])):
            back = negate(along)
            plus = shifted(coeff, along) * (shifted(field_pad, combine_shift(along, across, 1)) - shifted(field_pad, combine_shift(along, across, -1)))
            minus = shifted(coeff, back) * (shifted(field_pad, combine_shift(back, across, 1)) - shifted(field_pad, combine_shift(back, across, -1)))
            total = total + 0.25 * (plus - minus)
    return total


def sensitivities(field_pad, adjoint_pad, squares, crosses):
    centre_u = shifted(field_pad, (0, 0, 0))
    centre_l = shifted(adjoint_pad, (0, 0, 0))
    along_long = jnp.zeros_like(centre_u)
    along_trans = jnp.zeros_like(centre_u)
    for slot in range(3):
        unit = UNITS[slot]
        back = negate(unit)
        term = -0.5 * ((shifted(field_pad, unit) - centre_u) * (shifted(adjoint_pad, unit) - centre_l)
                       + (centre_u - shifted(field_pad, back)) * (centre_l - shifted(adjoint_pad, back)))
        along_long = along_long + term * squares[slot]
        along_trans = along_trans + term * (1.0 - squares[slot])
    for first, second, slot in PAIRS:
        term = -(central(adjoint_pad, UNITS[first]) * central(field_pad, UNITS[second])
                 + central(adjoint_pad, UNITS[second]) * central(field_pad, UNITS[first]))
        along_long = along_long + term * crosses[slot - 3]
        along_trans = along_trans - term * crosses[slot - 3]
    return along_long, along_trans


def expand_tiles(values, tile):
    sizes = values.shape
    wide = jnp.broadcast_to(values[:, None, :, None, :, None], (sizes[0], tile, sizes[1], tile, sizes[2], tile))
    return wide.reshape(sizes[0] * tile, sizes[1] * tile, sizes[2] * tile)


def tile_sums(field, tile):
    sizes = field.shape
    return field.reshape(sizes[0] // tile, tile, sizes[1] // tile, tile, sizes[2] // tile, tile).sum(axis=(1, 3, 5))


def region_table(tile_region, count):
    return (tile_region[..., None] == jnp.arange(count, dtype=jnp.int32)).astype(jnp.float32)


def reference(potential, recovery, fiber, sig_long, sig_trans, tile_region, tile_tissue, cot_potential, cot_recovery):
    tissue = tile_tissue.astype(jnp.float32)
    table = region_table(tile_region, sig_long.shape[0])
    slong = expand_tiles(jnp.sum(table * sig_long, axis=-1) * tissue, TILE)
    strans = expand_tiles(jnp.sum(table * sig_trans, axis=-1) * tissue, TILE)
    tensor_pad = jnp.pad(tensor_of(fiber[0], fiber[1], slong, strans), ((0, 0), (1, 1), (1, 1), (1, 1)))
    squares, crosses = fiber_parts(fiber[0], fiber[1])
    states = []
    field, slow = potential, recovery
    for step in range(STEPS):
        states.append((field, slow))
        lap = diffuse(jnp.pad(field, 1), tensor_pad)
        ionic = -KAPPA * field * (field - ALPHA) * (field - 1.0) - field * slow
        field, slow = (field + TIME_STEP * (lap + ionic),
                       slow + TIME_STEP * EPS_W * (-slow - KAPPA * field * (field - ALPHA - 1.0)))
    final_potential = field
    adjoint, adjoint_slow = cot_potential, cot_recovery
    total_long = jnp.zeros_like(potential)
    total_trans = jnp.zeros_like(potential)
    for step in range(STEPS - 1, -1, -1):
        field, slow = states[step]
        adjoint_pad = jnp.pad(adjoint, 1)
        part_long, part_trans = sensitivities(jnp.pad(field, 1), adjoint_pad, squares, crosses)
        total_long = total_long + part_long
        total_trans = total_trans + part_trans
        lap = diffuse(adjoint_pad, tensor_pad)
        slope = -KAPPA * (3.0 * field * field - 2.0 * (ALPHA + 1.0) * field + ALPHA) - slow
        adjoint, adjoint_slow = (adjoint + TIME_STEP * (lap + slope * adjoint) - TIME_STEP * EPS_W * KAPPA * (2.0 * field - ALPHA - 1.0) * adjoint_slow,
                                 adjoint_slow - TIME_STEP * field * adjoint - TIME_STEP * EPS_W * adjoint_slow)
    scale = TIME_STEP / (TILE ** 1.5)
    sums_long = tile_sums(total_long, TILE) * tissue * scale
    sums_trans = tile_sums(total_trans, TILE) * tissue * scale
    grad_long = jnp.sum(table * sums_long[..., None], axis=(0, 1, 2))
    grad_trans = jnp.sum(table * sums_trans[..., None], axis=(0, 1, 2))
    return final_potential, adjoint, grad_long, grad_trans
```

```python
import jax
import jax.numpy as jnp
from jax import lax
from jax.experimental import pallas as pl
from jax.experimental.pallas import tpu as pltpu
from jax.sharding import PartitionSpec as P

MESH = pl.DeviceIdType.MESH
STEPS = 4
DT = 0.05
EPS_W = 0.1
NX, NY, ZL = 32, 32, 128
Y0 = 8
YP = 48
YT = NY // 8
TILE = 32

XX, XY, XZ, YZ, YY, ZZ = range(6)

SIN = (0.9999999954376937, -0.16666657521871267, 0.008333039791882324, -0.0001980823258586027, 2.603293610558432e-06)
COS = (
    0.9999999997626233,
    -0.4999999931520218,
    0.041666634639589036,
    -0.0013888340619260778,
    2.4759088421126325e-05,
    -2.6032335044441285e-07,
)


def poly(z, coefs):
    total = coefs[-1] * z + coefs[-2]
    for value in coefs[-3::-1]:
        total = total * z + value
    return total


def sincos(x):
    t = (1.5707963705062866 - jnp.abs(x)) - 4.371139000186241e-08
    z = t * t
    cosine = t * poly(z, SIN)
    size = poly(z, COS)
    return jnp.where(x < 0.0, -size, size), cosine


def products(theta, phi):
    st, ct = sincos(theta)
    sp, cp = sincos(phi)
    fx, fy, fz = cp * ct, cp * st, sp
    return {XX: fx * fx, YY: fy * fy, ZZ: fz * fz, XY: fx * fy, XZ: fx * fz, YZ: fy * fz}


def lane():
    return lax.broadcasted_iota(jnp.int32, (8, ZL), 1)


def z_up(h0, h1):
    last = lane() == ZL - 1
    r0, r1 = pltpu.roll(h0, ZL - 1, 1), pltpu.roll(h1, ZL - 1, 1)
    return jnp.where(last, r1, r0), jnp.where(last, 0.0, r1)


def z_down(h0, h1, edge=0.0):
    first = lane() == 0
    r0, r1 = pltpu.roll(h0, 1, 1), pltpu.roll(h1, 1, 1)
    return jnp.where(first, edge, r0), jnp.where(first, r0, r1)


def pair(fn):
    return fn(0), fn(1)


def kernel(
    gx_count,
    gy_count,
    pot,
    rec,
    fib,
    cot_p,
    cot_r,
    sig_l,
    sig_t,
    region,
    tissue,
    out_u,
    out_lam,
    out_l,
    out_t,
    u0,
    u1,
    u2,
    u3,
    l4,
    l3,
    l2,
    l1,
    ulast,
    llast,
    w0,
    w1,
    w2,
    w3,
    mu,
    fp,
    dx,
    dy,
    dz,
    dzm,
    ex,
    tt,
    bb,
    py,
    ay,
    ysend,
    yrecv,
    crecv,
    fysend,
    fyrecv,
    eyh,
    dyh,
    pk,
    tinfo,
    trecv,
    g1send,
    g1recv,
    quad,
    rsend,
    rrecv,
    rg,
    sv,
    acc,
    load_sem,
    xs,
    xr,
    fs,
    fr,
    ts,
    tr,
    g1s,
    g1r,
    g2s,
    g2r,
    r1s,
    r1r,
    r2s,
    r2r,
):
    gx, gy = lax.axis_index("gx"), lax.axis_index("gy")
    has = {"l": gx > 0, "r": gx < gx_count - 1, "d": gy > 0, "u": gy < gy_count - 1}
    us = (u0, u1, u2, u3)
    ls = (l4, l3, l2, l1)
    ws = (w0, w1, w2, w3)
    fields = us + ls

    def loads(index, src, dst, padded):
        out = []
        for h in range(2):
            s = src.at[:, :, pl.ds(h * ZL, ZL)]
            d = dst.at[pl.ds(1, NX), h, pl.ds(Y0, NY), :] if padded else dst.at[:, h]
            out.append(pltpu.make_async_copy(s, d, load_sem.at[index, h]))
        return out

    copies = [
        loads(0, pot, u0, True),
        loads(1, cot_p, l4, True),
        loads(2, fib.at[0], tt, False),
        loads(3, fib.at[1], bb, True),
        loads(4, rec, w0, False),
        loads(5, cot_r, mu, False),
    ]
    for group in copies:
        for copy in group:
            copy.start()

    barrier = pltpu.get_barrier_semaphore()

    @pl.loop(1, gx_count)
    def _(k):
        pl.semaphore_signal(barrier, inc=1, device_id=(lax.rem(gx + k, gx_count), gy), device_id_type=MESH)

    @pl.loop(1, gy_count)
    def _(k):
        pl.semaphore_signal(barrier, inc=1, device_id=(gx, lax.rem(gy + k, gy_count)), device_id_type=MESH)

    corner_list = (("l", "d"), ("l", "u"), ("r", "d"), ("r", "u"))
    step_of = {"l": (-1, 0), "r": (1, 0), "d": (0, -1), "u": (0, 1)}

    def both(a, b):
        return jnp.logical_and(has[a], has[b])

    def target(*sides):
        return (gx + sum(step_of[s][0] for s in sides), gy + sum(step_of[s][1] for s in sides))

    for a, b in corner_list:

        @pl.when(both(a, b))
        def _(a=a, b=b):
            pl.semaphore_signal(barrier, inc=1, device_id=target(a, b), device_id_type=MESH)

    gxi = (gx > 0).astype(jnp.int32) + (gx < gx_count - 1).astype(jnp.int32)
    gyi = (gy > 0).astype(jnp.int32) + (gy < gy_count - 1).astype(jnp.int32)

    @pl.when(jnp.logical_not(has["l"]))
    def _():
        for f in fields:
            f[0, :, Y0 : Y0 + NY, :] = jnp.zeros((2, NY, ZL), jnp.float32)
        for c in (XX, XY, XZ):
            fp[c, 0, :, Y0 : Y0 + NY, :] = jnp.zeros((2, NY, ZL), jnp.float32)
        trecv[0] = jnp.zeros((8, ZL), jnp.float32)

    @pl.when(jnp.logical_not(has["r"]))
    def _():
        for f in fields:
            f[NX + 1, :, Y0 : Y0 + NY, :] = jnp.zeros((2, NY, ZL), jnp.float32)
        for c in (XX, XY, XZ):
            fp[c, NX + 1, :, Y0 : Y0 + NY, :] = jnp.zeros((2, NY, ZL), jnp.float32)
        trecv[1] = jnp.zeros((8, ZL), jnp.float32)

    for side, name in enumerate("du"):

        @pl.when(jnp.logical_not(has[name]))
        def _(side=side):
            for k in range(8):
                yrecv[k, side, :, Y0 : Y0 + NY, :] = jnp.zeros((2, NY, ZL), jnp.float32)
            fyrecv[side] = jnp.zeros((3, 2, NX, ZL), jnp.float32)
            trecv[2 + side] = jnp.zeros((8, ZL), jnp.float32)

    for c, (a, b) in enumerate(corner_list):

        @pl.when(jnp.logical_not(both(a, b)))
        def _(c=c):
            for k in range(8):
                crecv[k, c] = jnp.zeros((2, 8, ZL), jnp.float32)

    pl.semaphore_wait(barrier, gx_count - 1 + gy_count - 1 + gxi * gyi)

    def remote(src, dst, send, recv, device):
        return pltpu.make_async_remote_copy(
            src_ref=src, dst_ref=dst, send_sem=send, recv_sem=recv, device_id=device, device_id_type=MESH
        )

    lanes = lane()
    tile_of = lanes // TILE

    def lane_vector(ref, h):
        value = jnp.zeros((8, ZL), jnp.float32)
        for k in range(4):
            value = jnp.where(tile_of == k, ref[0, 0, 4 * h + k].astype(jnp.float32), value)
        return value

    own_r = [lane_vector(region, h) for h in range(2)]
    own_t = [lane_vector(tissue, h) for h in range(2)]
    sub = lax.broadcasted_iota(jnp.int32, (8, ZL), 0)
    subf = sub.astype(jnp.float32)
    tinfo[...] = jnp.where(
        sub == 0, own_r[0], jnp.where(sub == 1, own_r[1], jnp.where(sub == 2, own_t[0], own_t[1]))
    )
    opposite = {"l": 1, "r": 0, "d": 3, "u": 2}
    names = "lrdu"

    def tile_copies():
        return [
            (
                has[s],
                has[names[opposite[s]]],
                remote(tinfo, trecv.at[opposite[s]], ts.at[i], tr.at[opposite[s]], target(s)),
            )
            for i, s in enumerate(names)
        ]

    def start(list_):
        for cond, _, copy in list_:

            @pl.when(cond)
            def _(copy=copy):
                copy.start()

    def wait_recv(list_):
        for _, cond, copy in list_:

            @pl.when(cond)
            def _(copy=copy):
                copy.wait_recv()

    def wait_send(list_):
        for cond, _, copy in list_:

            @pl.when(cond)
            def _(copy=copy):
                copy.wait_send()

    start(tile_copies())

    value = jnp.where(
        lanes < 64, jnp.where(sub == 2 * gy, sig_l[0], sig_l[1]), jnp.where(sub == 2 * gy, sig_t[0], sig_t[1])
    )
    mine = jnp.where(jnp.logical_or(sub == 2 * gy, sub == 2 * gy + 1), value, 0.0)
    g1send[...] = mine

    def g1(k):
        return remote(g1send, g1recv.at[k], g1s.at[k], g1r.at[k], (gx, lax.rem(gy + k, gy_count)))

    for k in range(1, gy_count):
        g1(k).start()

    def exchange(k):
        f = fields[k]
        rows = pl.ds(Y0, NY)
        out = [
            (has["l"], has["r"], remote(f.at[1, :, rows, :], f.at[NX + 1, :, rows, :], xs.at[k, 0], xr.at[k, 1], target("l"))),
            (has["r"], has["l"], remote(f.at[NX, :, rows, :], f.at[0, :, rows, :], xs.at[k, 1], xr.at[k, 0], target("r"))),
            (has["d"], has["u"], remote(ysend.at[k, 0], yrecv.at[k, 1, :, rows, :], xs.at[k, 2], xr.at[k, 3], target("d"))),
            (has["u"], has["d"], remote(ysend.at[k, 1], yrecv.at[k, 0, :, rows, :], xs.at[k, 3], xr.at[k, 2], target("u"))),
        ]
        for c, (a, b) in enumerate(corner_list):
            xrow = 0 if a == "l" else NX - 8
            src = ysend.at[k, 0 if b == "d" else 1, :, pl.ds(xrow, 8), :]
            out.append((both(a, b), both(*corner_list[3 - c]), remote(src, crecv.at[k, 3 - c], xs.at[k, 4 + c], xr.at[k, 7 - c], target(a, b))))
        return out

    def wait_load(index):
        for copy in copies[index]:
            copy.wait()

    def pack_rows(f, k):
        @pl.loop(0, NX)
        def _(x):
            for h in range(2):
                ysend[k, 0, h, pl.ds(x, 1), :] = f[x + 1, h, Y0 : Y0 + 1, :]
                ysend[k, 1, h, pl.ds(x, 1), :] = f[x + 1, h, Y0 + NY - 1 : Y0 + NY, :]

    wait_load(0)
    pack_rows(u0, 0)
    start(exchange(0))
    wait_load(1)
    pack_rows(l4, 4)
    start(exchange(4))

    quad_own = mine
    for k in range(1, gy_count):
        g1(k).wait_recv()
        quad_own = quad_own + g1recv[k]
    quad[0] = quad_own

    def g2(k):
        return remote(quad.at[0], quad.at[k], g2s, g2r, (lax.rem(gx + k, gx_count), gy))

    @pl.loop(1, gx_count)
    def _(k):
        g2(k).start()

    wait_load(2)
    wait_load(3)

    def trig(x):
        for yt in range(YT):
            y = yt * 8
            for h in range(2):
                got = products(tt[x, h, y : y + 8, :], bb[x + 1, h, Y0 + y : Y0 + y + 8, :])
                for c in range(6):
                    fp[c, x + 1, h, Y0 + y : Y0 + y + 8, :] = got[c]
                for i, c in enumerate((XY, YZ, YY)):
                    if yt == 0:
                        fysend[0, i, h, pl.ds(x, 1), :] = got[c][0:1]
                    if yt == YT - 1:
                        fysend[1, i, h, pl.ds(x, 1), :] = got[c][7:8]

    pl.loop(0, NX)(trig)

    def fiber_exchange():
        rows = pl.ds(Y0, NY)
        return [
            (has["l"], has["r"], remote(fp.at[pl.ds(0, 3), 1, :, rows, :], fp.at[pl.ds(0, 3), NX + 1, :, rows, :], fs.at[0], fr.at[1], target("l"))),
            (has["r"], has["l"], remote(fp.at[pl.ds(0, 3), NX, :, rows, :], fp.at[pl.ds(0, 3), 0, :, rows, :], fs.at[1], fr.at[0], target("r"))),
            (has["d"], has["u"], remote(fysend.at[0], fyrecv.at[1], fs.at[2], fr.at[3], target("d"))),
            (has["u"], has["d"], remote(fysend.at[1], fyrecv.at[0], fs.at[3], fr.at[2], target("u"))),
        ]

    start(fiber_exchange())

    wait_recv(tile_copies())
    remote(quad.at[pl.ds(1, gx_count - 1)], quad.at[pl.ds(1, gx_count - 1)], g2s, g2r, (gx, gy)).wait_recv()
    regions = list(own_r)
    flags = list(own_t)
    for i in range(4):
        for h in range(2):
            regions.append(jnp.broadcast_to(trecv[i, h : h + 1, :], (8, ZL)))
            flags.append(jnp.broadcast_to(trecv[i, 2 + h : 3 + h, :], (8, ZL)))

    def lookup(k, sums):
        tile = quad[k]
        turned = pltpu.roll(tile, 64, 1)
        low = lanes < 64
        long_, trans = jnp.where(low, tile, turned), jnp.where(low, turned, tile)
        group = lax.rem(gx - k + gx_count, gx_count)
        ids = subf + (8 * group).astype(jnp.float32)
        new = []
        for i in range(10):
            hit = regions[i] == ids
            new.append(sums[2 * i] + jnp.where(hit, long_, 0.0))
            new.append(sums[2 * i + 1] + jnp.where(hit, trans, 0.0))
        return tuple(new)

    sums = lax.fori_loop(0, gx_count, lookup, tuple(jnp.zeros((8, ZL), jnp.float32) for _ in range(20)))
    for i in range(10):
        s_l = jnp.broadcast_to(jnp.sum(sums[2 * i], axis=0, keepdims=True), (8, ZL)) * flags[i]
        s_t = jnp.broadcast_to(jnp.sum(sums[2 * i + 1], axis=0, keepdims=True), (8, ZL)) * flags[i]
        sv[i // 2, 0, i % 2] = s_t
        sv[i // 2, 1, i % 2] = s_l - s_t

    wait_recv(fiber_exchange())
    c_pair = 0.25 * DT
    c_axis = 0.5 * DT
    st = pair(lambda h: sv[0, 0, h])
    ee = pair(lambda h: sv[0, 1, h])
    ea = pair(lambda h: c_axis * ee[h])
    ep = pair(lambda h: c_pair * ee[h])
    s2 = pair(lambda h: DT * st[h])

    def coefficients(p):
        for yt in range(YT):
            y = yt * 8
            r = slice(Y0 + y, Y0 + y + 8)
            dzz = []
            for h in range(2):
                q = slice(y, y + 8)
                dx[p, h, q, :] = s2[h] + ea[h] * (fp[XX, p, h, r, :] + fp[XX, p + 1, h, r, :])
                up = fp[YY, p, h, Y0 + y + 1 : Y0 + y + 9, :]
                dy[p, h, q, :] = s2[h] + ea[h] * (fp[YY, p, h, r, :] + up)
                dzz.append(c_axis * st[h] + ea[h] * fp[ZZ, p, h, r, :])
                for i, c in enumerate((XY, XZ, YZ)):
                    ex[i, p, h, q, :] = ep[h] * fp[c, p, h, r, :]
            up = z_up(*dzz)
            for h in range(2):
                dz[p, h, y : y + 8, :] = dzz[h] + up[h]
            dzm[p, y : y + 8, :] = dzz[0]

    pl.loop(1, NX + 1)(coefficients)
    for side, plane, inner in ((0, 0, 1), (1, NX + 1, NX)):
        for h in range(2):
            st_n, e_n = sv[1 + side, 0, h], sv[1 + side, 1, h]
            for yt in range(YT):
                q = slice(yt * 8, yt * 8 + 8)
                r = slice(Y0 + yt * 8, Y0 + yt * 8 + 8)
                total = (st_n + e_n * fp[XX, plane, h, r, :]) + (st[h] + ee[h] * fp[XX, inner, h, r, :])
                dx[0 if side == 0 else NX, h, q, :] = c_axis * total
                for i, c in enumerate((XY, XZ)):
                    ex[i, plane, h, q, :] = c_pair * e_n * fp[c, plane, h, r, :]
    for side in range(2):
        for h in range(2):
            st_n, e_n = sv[3 + side, 0, h], sv[3 + side, 1, h]
            for t in range(NX // 8):
                q = slice(t * 8, t * 8 + 8)
                total = (st_n + e_n * fyrecv[side, 2, h, q, :]) + (st[h] + ee[h] * fysend[side, 2, h, q, :])
                dyh[side, h, q, :] = c_axis * total
                for i in range(2):
                    eyh[side, i, h, q, :] = c_pair * e_n * fyrecv[side, i, h, q, :]

    @pl.loop(0, NX)
    def _(x):
        for h in range(2):
            dy[x + 1, h, NY - 1 : NY, :] = dyh[1, h, pl.ds(x, 1), :]

    acc[...] = jnp.zeros_like(acc)

    def install(k):
        f = fields[k]
        for c, (a, b) in enumerate(corner_list):
            plane = 0 if a == "l" else NX + 1
            row = Y0 - 1 if b == "d" else Y0 + NY
            side = 0 if b == "d" else 1
            edge = Y0 - 1 if a == "l" else Y0 + NX
            at = 7 if a == "l" else 0
            for h in range(2):
                v = crecv[k, c, h, at : at + 1, :]
                f[plane, h, row : row + 1, :] = v
                yrecv[k, side, h, edge : edge + 1, :] = v
        for side in range(2):
            for t in range(NX // 8):
                q = slice(t * 8, t * 8 + 8)
                r = slice(Y0 + t * 8, Y0 + t * 8 + 8)
                c = pair(lambda h: yrecv[k, side, h, r, :])
                zp, zm = z_up(*c), z_down(*c)
                for h in range(2):
                    g_x = yrecv[k, side, h, Y0 + t * 8 + 1 : Y0 + t * 8 + 9, :] - yrecv[k, side, h, Y0 + t * 8 - 1 : Y0 + t * 8 + 7, :]
                    flux = eyh[side, 0, h, q, :] * g_x + eyh[side, 1, h, q, :] * (zp[h] - zm[h])
                    if side == 0:
                        flux = flux + dyh[0, h, q, :] * (ysend[k, 0, h, q, :] - c[h])
                    pk[side, h, q, :] = flux

        @pl.loop(0, NX)
        def _(x):
            for h in range(2):
                f[x + 1, h, Y0 - 1 : Y0, :] = yrecv[k, 0, h, pl.ds(x + Y0, 1), :]
                f[x + 1, h, Y0 + NY : Y0 + NY + 1, :] = yrecv[k, 1, h, pl.ds(x + Y0, 1), :]
                ay[x + 1, h, Y0 - 1 : Y0, :] = pk[0, h, pl.ds(x, 1), :]
                py[x + 1, h, Y0 + NY : Y0 + NY + 1, :] = pk[1, h, pl.ds(x, 1), :]

    def rows(y, shift=0):
        return slice(Y0 + y + shift, Y0 + y + shift + 8)

    def edge_flux(f, p, yt):
        y = yt * 8
        q = slice(y, y + 8)
        c = pair(lambda h: f[p, h, rows(y), :])
        zp, zm = z_up(*c), z_down(*c)
        out = []
        for h in range(2):
            g_y = f[p, h, rows(y, 1), :] - f[p, h, rows(y, -1), :]
            out.append(ex[0, p, h, q, :] * g_y + ex[1, p, h, q, :] * (zp[h] - zm[h]))
        return c, out

    def before(f):
        for yt in range(YT):
            y = yt * 8
            c, flux = edge_flux(f, 0, yt)
            for h in range(2):
                bb[0, h, rows(y), :] = flux[h] + dx[0, h, y : y + 8, :] * (f[1, h, rows(y), :] - c[h])

    def stage_a(f, p, yt, react):
        y = yt * 8
        q = slice(y, y + 8)
        c = pair(lambda h: f[p, h, rows(y), :])
        xp = pair(lambda h: f[p + 1, h, rows(y), :])
        xm = pair(lambda h: f[p - 1, h, rows(y), :])
        yp = pair(lambda h: f[p, h, rows(y, 1), :])
        ym = pair(lambda h: f[p, h, rows(y, -1), :])
        zp, zm = z_up(*c), z_down(*c)
        own = react(p, y, c)
        flux_x, local, pz, az = [], [], [], []
        for h in range(2):
            e_xy, e_xz, e_yz = (ex[i, p, h, q, :] for i in range(3))
            g_x, g_y, g_z = xp[h] - xm[h], yp[h] - ym[h], zp[h] - zm[h]
            p_x = e_xy * g_y + e_xz * g_z
            p_y = e_xy * g_x + e_yz * g_z
            p_z = e_xz * g_x + e_yz * g_y
            f_x = dx[p, h, q, :] * (xp[h] - c[h])
            f_y = dy[p, h, q, :] * (yp[h] - c[h])
            f_z = dz[p, h, q, :] * (zp[h] - c[h])
            back = bb[p - 1, h, rows(y), :]
            bb[p, h, rows(y), :] = f_x + p_x
            py[p, h, rows(y), :] = p_y
            ay[p, h, rows(y), :] = f_y + p_y
            pz.append(p_z)
            az.append(f_z + p_z)
            flux_x.append(p_x)
            local.append((own[h] + f_x) + (f_y + f_z) - back)
        up = z_up(*pz)
        down = z_down(*az, edge=dzm[p, q, :] * c[0])
        for h in range(2):
            tt[p - 1, h, q, :] = local[h] + (up[h] - down[h])
        return flux_x

    def stage_b(p, yt, flux_x, put):
        y = yt * 8
        for h in range(2):
            value = (tt[p - 1, h, y : y + 8, :] + flux_x[h]) + (py[p, h, rows(y, 1), :] - ay[p, h, rows(y, -1), :])
            put(p, h, yt, value)

    def apply(k, react, put):
        f = fields[k]
        before(f)
        for yt in range(YT):
            stage_a(f, 1, yt, react)

        @pl.loop(2, NX + 1)
        def _(p):
            for yt in range(YT):
                stage_b(p - 1, yt, stage_a(f, p, yt, react), put)

        for yt in range(YT):
            stage_b(NX, yt, edge_flux(f, NX + 1, yt)[1], put)

    def put_field(k):
        f = fields[k]

        def put(p, h, yt, value):
            f[p, h, rows(yt * 8), :] = value
            if yt == 0:
                ysend[k, 0, h, pl.ds(p - 1, 1), :] = value[0:1]
            if yt == YT - 1:
                ysend[k, 1, h, pl.ds(p - 1, 1), :] = value[7:8]

        return put

    def put_last(ref):
        def put(p, h, yt, value):
            ref[p - 1, h, yt * 8 : yt * 8 + 8, :] = value

        return put

    def store(ref, out, index):
        return [
            pltpu.make_async_copy(ref.at[:, h], out.at[:, :, pl.ds(h * ZL, ZL)], load_sem.at[index, h]) for h in range(2)
        ]

    wait_load(4)
    wait_load(5)
    for n in range(STEPS):
        wait_recv(exchange(n))
        install(n)

        def react(p, y, c, n=n):
            q = slice(y, y + 8)
            out = []
            for h in range(2):
                w = ws[n][p - 1, h, q, :]
                u = c[h]
                rate = (1.0 - DT * w) - (u - 0.15) * (8.0 * DT * u - 8.0 * DT)
                out.append(u * rate)
                if n < STEPS - 1:
                    ws[n + 1][p - 1, h, q, :] = (1.0 - DT * EPS_W) * w - u * (
                        8.0 * DT * EPS_W * u - 8.0 * DT * EPS_W * 1.15
                    )
            return out

        apply(n, react, put_field(n + 1) if n < STEPS - 1 else put_last(ulast))
        if n < STEPS - 1:
            start(exchange(n + 1))
    for copy in store(ulast, out_u, 0):
        copy.start()

    def sens(n, k):
        u, lam = us[n], fields[k]

        def body(p, sums):
            total_l, total_t = [sums[0], sums[1]], [sums[2], sums[3]]
            for yt in range(YT):
                y = yt * 8
                both_ = []
                for f in (u, lam):
                    c = pair(lambda h: f[p, h, rows(y), :])
                    zp, zm = z_up(*c), z_down(*c)
                    parts = []
                    for h in range(2):
                        near = (
                            (f[p + 1, h, rows(y), :], f[p - 1, h, rows(y), :]),
                            (f[p, h, rows(y, 1), :], f[p, h, rows(y, -1), :]),
                            (zp[h], zm[h]),
                        )
                        parts.append([(b - c[h], c[h] - a, b - a) for b, a in near])
                    both_.append(parts)
                for h in range(2):
                    (ux, uy, uz), (lx, ly, lz) = both_[0][h], both_[1][h]
                    m = [a[0] * b[0] + a[1] * b[1] for a, b in ((ux, lx), (uy, ly), (uz, lz))]
                    f_xx, f_xy, f_xz, f_yz, f_yy, f_zz = (fp[c, p, h, rows(y), :] for c in range(6))
                    cross = (
                        ux[2] * (f_xy * ly[2] + f_xz * lz[2])
                        + uy[2] * (f_xy * lx[2] + f_yz * lz[2])
                        + uz[2] * (f_xz * lx[2] + f_yz * ly[2])
                    )
                    total_l[h] = total_l[h] + ((m[0] * f_xx + m[1] * f_yy) + (m[2] * f_zz + 0.5 * cross))
                    total_t[h] = total_t[h] + (m[0] + m[1] + m[2])
            return (*total_l, *total_t)

        zero = jnp.zeros((8, ZL), jnp.float32)
        sums = lax.fori_loop(1, NX + 1, body, (zero,) * 4)
        for i in range(4):
            acc[i] = acc[i] + sums[i]

    def adjoint(n, k, put):
        def react(p, y, c):
            q = slice(y, y + 8)
            out = []
            for h in range(2):
                u = us[n][p, h, rows(y), :]
                w = ws[n][p - 1, h, q, :]
                m = mu[p - 1, h, q, :]
                rate = (1.0 - 8.0 * DT * 0.15) + u * (8.0 * DT * 2.3 - 24.0 * DT * u) - DT * w
                out.append(c[h] * rate - (16.0 * DT * EPS_W * u - 8.0 * DT * EPS_W * 1.15) * m)
                if n > 0:
                    mu[p - 1, h, q, :] = (1.0 - DT * EPS_W) * m - DT * u * c[h]
            return out

        apply(k, react, put)

    for n in range(STEPS - 1, 0, -1):
        k = 4 + STEPS - 1 - n
        wait_recv(exchange(k))
        install(k)
        adjoint(n, k, put_field(k + 1))
        start(exchange(k + 1))
        sens(n, k)
    wait_recv(exchange(7))
    install(7)
    sens(0, 7)

    scale = -0.5 * DT / TILE**1.5
    flat = []
    for h in range(2):
        s_l = jnp.broadcast_to(jnp.sum(acc[h], axis=0, keepdims=True), (8, ZL))
        s_a = jnp.broadcast_to(jnp.sum(acc[2 + h], axis=0, keepdims=True), (8, ZL))
        flat.append((scale * own_t[h] * s_l, scale * own_t[h] * (s_a - s_l)))

    def parts_of(group):
        ids = subf + (8 * group).astype(jnp.float32)
        tot = []
        for j in range(2):
            v = sum(jnp.where(own_r[h] == ids, flat[h][j], 0.0) for h in range(2))
            tot.append(v + pltpu.roll(v, 64, 1))
        return jnp.where(lanes < 64, tot[0], tot[1])

    rrecv[0] = parts_of(gx)

    def r1(k):
        return remote(rsend.at[k], rrecv.at[k], r1s, r1r, (lax.rem(gx + k, gx_count), gy))

    @pl.loop(1, gx_count)
    def _(k):
        rsend[k] = parts_of(lax.rem(gx + k, gx_count))
        r1(k).start()

    adjoint(0, 7, put_last(llast))
    for copy in store(llast, out_lam, 1):
        copy.start()

    remote(rsend.at[pl.ds(1, gx_count - 1)], rrecv.at[pl.ds(1, gx_count - 1)], r1s, r1r, (gx, gy)).wait_recv()
    total = lax.fori_loop(0, gx_count, lambda k, s: s + rrecv[k], jnp.zeros((8, ZL), jnp.float32))
    rg[0] = total

    def r2(k):
        return remote(rg.at[0], rg.at[k], r2s.at[k], r2r.at[k], (gx, lax.rem(gy + k, gy_count)))

    for k in range(1, gy_count):
        r2(k).start()
    for k in range(1, gy_count):
        r2(k).wait_recv()
        total = total + rg[k]
    for j in range(2):
        mine_row = sub == 2 * gy + j
        out_l[j] = jnp.sum(jnp.where(jnp.logical_and(mine_row, lanes < 64), total, 0.0))
        out_t[j] = jnp.sum(jnp.where(jnp.logical_and(mine_row, lanes >= 64), total, 0.0))

    wait_send(tile_copies())
    wait_send(fiber_exchange())
    for k in range(8):
        wait_send(exchange(k))
    for k in range(1, gy_count):
        g1(k).wait_send()
        r2(k).wait_send()
    remote(quad.at[pl.ds(1, gx_count - 1)], quad.at[pl.ds(1, gx_count - 1)], g2s, g2r, (gx, gy)).wait_send()
    remote(rsend.at[pl.ds(1, gx_count - 1)], rrecv.at[pl.ds(1, gx_count - 1)], r1s, r1r, (gx, gy)).wait_send()
    for copy in store(ulast, out_u, 0) + store(llast, out_lam, 1):
        copy.wait()


def solution(mesh):
    gx_count, gy_count = mesh.shape["gx"], mesh.shape["gy"]

    def local(*args):
        any_, smem = pl.BlockSpec(memory_space=pl.ANY), pl.BlockSpec(memory_space=pltpu.SMEM)
        f32 = jnp.float32
        padded = pltpu.VMEM((NX + 2, 2, YP, ZL), f32)
        plain = pltpu.VMEM((NX, 2, NY, ZL), f32)
        dma = pltpu.SemaphoreType.DMA
        scratch = [padded] * 8 + [plain] * 2 + [plain] * 4 + [plain]
        scratch += [
            pltpu.VMEM((6, NX + 2, 2, YP, ZL), f32),
            pltpu.VMEM((NX + 1, 2, NY, ZL), f32),
            pltpu.VMEM((NX + 1, 2, NY, ZL), f32),
            pltpu.VMEM((NX + 1, 2, NY, ZL), f32),
            pltpu.VMEM((NX + 1, NY, ZL), f32),
            pltpu.VMEM((3, NX + 2, 2, NY, ZL), f32),
            plain,
            padded,
            padded,
            padded,
            pltpu.VMEM((8, 2, 2, NX, ZL), f32),
            pltpu.VMEM((8, 2, 2, YP, ZL), f32),
            pltpu.VMEM((8, 4, 2, 8, ZL), f32),
            pltpu.VMEM((2, 3, 2, NX, ZL), f32),
            pltpu.VMEM((2, 3, 2, NX, ZL), f32),
            pltpu.VMEM((2, 2, 2, NX, ZL), f32),
            pltpu.VMEM((2, 2, NX, ZL), f32),
            pltpu.VMEM((2, 2, NX, ZL), f32),
            pltpu.VMEM((8, ZL), f32),
            pltpu.VMEM((4, 8, ZL), f32),
            pltpu.VMEM((8, ZL), f32),
            pltpu.VMEM((gy_count, 8, ZL), f32),
            pltpu.VMEM((gx_count, 8, ZL), f32),
            pltpu.VMEM((gx_count, 8, ZL), f32),
            pltpu.VMEM((gx_count, 8, ZL), f32),
            pltpu.VMEM((gy_count, 8, ZL), f32),
            pltpu.VMEM((5, 2, 2, 8, ZL), f32),
            pltpu.VMEM((4, 8, ZL), f32),
            dma((6, 2)),
            dma((8, 8)),
            dma((8, 8)),
            dma((4,)),
            dma((4,)),
            dma((4,)),
            dma((4,)),
            dma((gy_count,)),
            dma((gy_count,)),
            dma(()),
            dma(()),
            dma(()),
            dma(()),
            dma((gy_count,)),
            dma((gy_count,)),
        ]
        field = jax.ShapeDtypeStruct((NX, NY, 2 * ZL), f32)
        two = jax.ShapeDtypeStruct((2,), f32)

        def body(*refs):
            kernel(gx_count, gy_count, *refs)

        return pl.pallas_call(
            body,
            out_shape=(field, field, two, two),
            in_specs=[any_] * 5 + [smem] * 4,
            out_specs=(any_, any_, smem, smem),
            scratch_shapes=scratch,
            compiler_params=pltpu.CompilerParams(
                collective_id=0, has_side_effects=True, vmem_limit_bytes=60 * 1024 * 1024
            ),
        )(*args[:3], *args[7:], *args[3:7])

    return jax.shard_map(
        local,
        mesh=mesh,
        in_specs=(
            P("gx", "gy", None),
            P("gx", "gy", None),
            P(None, "gx", "gy", None),
            P(("gx", "gy")),
            P(("gx", "gy")),
            P("gx", "gy", None),
            P("gx", "gy", None),
            P("gx", "gy", None),
            P("gx", "gy", None),
        ),
        out_specs=(P("gx", "gy", None), P("gx", "gy", None), P(("gx", "gy")), P(("gx", "gy"))),
        check_vma=False,
    )
```

```python
import jax
import jax.numpy as jnp
from jax import lax
from jax.experimental import pallas as pl
from jax.experimental.pallas import tpu as pltpu
from jax.sharding import PartitionSpec as P

MESH = pl.DeviceIdType.MESH
STEPS = 4
DT = 0.05
EPS_W = 0.1
NX, NY, ZL = 32, 32, 128
Y0 = 8
YP = 48
YT = NY // 8
TILE = 32

XX, XY, XZ, YZ, YY, ZZ = range(6)

SIN = (0.9999999954376937, -0.16666657521871267, 0.008333039791882324, -0.0001980823258586027, 2.603293610558432e-06)
COS = (
    0.9999999997626233,
    -0.4999999931520218,
    0.041666634639589036,
    -0.0013888340619260778,
    2.4759088421126325e-05,
    -2.6032335044441285e-07,
)


def poly(z, coefs):
    total = coefs[-1] * z + coefs[-2]
    for value in coefs[-3::-1]:
        total = total * z + value
    return total


def sincos(x):
    t = (1.5707963705062866 - jnp.abs(x)) - 4.371139000186241e-08
    z = t * t
    cosine = t * poly(z, SIN)
    size = poly(z, COS)
    return jnp.where(x < 0.0, -size, size), cosine


def products(theta, phi):
    st, ct = sincos(theta)
    sp, cp = sincos(phi)
    fx, fy, fz = cp * ct, cp * st, sp
    return {XX: fx * fx, YY: fy * fy, ZZ: fz * fz, XY: fx * fy, XZ: fx * fz, YZ: fy * fz}


def lane():
    return lax.broadcasted_iota(jnp.int32, (8, ZL), 1)


def z_up(h0, h1):
    last = lane() == ZL - 1
    r0, r1 = pltpu.roll(h0, ZL - 1, 1), pltpu.roll(h1, ZL - 1, 1)
    return jnp.where(last, r1, r0), jnp.where(last, 0.0, r1)


def z_down(h0, h1, edge=0.0):
    first = lane() == 0
    r0, r1 = pltpu.roll(h0, 1, 1), pltpu.roll(h1, 1, 1)
    return jnp.where(first, edge, r0), jnp.where(first, r0, r1)


def pair(fn):
    return fn(0), fn(1)


def kernel(
    gx_count,
    gy_count,
    pot,
    rec,
    fib,
    cot_p,
    cot_r,
    sig_l_in,
    sig_t_in,
    region_in,
    tissue_in,
    out_u,
    out_lam,
    out_l,
    out_t,
    u0,
    u1,
    u2,
    u3,
    l4,
    l3,
    l2,
    l1,
    ulast,
    llast,
    r0,
    r1_,
    r2_,
    r3,
    ww,
    mu,
    fp,
    dx,
    dy,
    dz,
    dzm,
    ex,
    fhx,
    fhy,
    tt,
    bb,
    py,
    ay,
    ysend,
    halo,
    crecv,
    fysend,
    frecv,
    cfd,
    cfh,
    cfo,
    tinfo,
    trecv,
    g1send,
    g1recv,
    quad,
    rsend,
    rrecv,
    rg,
    sv,
    acc,
    sig_l,
    sig_t,
    region,
    tissue,
    load_sem,
    small_sem,
    xs,
    xr,
    fs,
    fr,
    ts,
    tr,
    g1s,
    g1r,
    g2s,
    g2r,
    r1s,
    r1r,
    r2s,
    r2r,
):
    gx, gy = lax.axis_index("gx"), lax.axis_index("gy")
    has = {"l": gx > 0, "r": gx < gx_count - 1, "d": gy > 0, "u": gy < gy_count - 1}
    us = (u0, u1, u2, u3)
    ls = (l4, l3, l2, l1)
    rs = (r0, r1_, r2_, r3)
    fields = us + ls
    data = pl.ds(Y0, NY)
    names = "lrdu"
    corner_list = (("l", "d"), ("l", "u"), ("r", "d"), ("r", "u"))
    step_of = {"l": (-1, 0), "r": (1, 0), "d": (0, -1), "u": (0, 1)}

    def loads(index, src, dst, padded):
        out = []
        for h in range(2):
            s = src.at[:, :, pl.ds(h * ZL, ZL)]
            d = dst.at[pl.ds(1, NX), h, data, :] if padded else dst.at[:, h]
            out.append(pltpu.make_async_copy(s, d, load_sem.at[index, h]))
        return out

    copies = [
        loads(0, fib.at[0], tt, False),
        loads(1, fib.at[1], bb, True),
        loads(2, pot, u0, True),
        loads(3, cot_p, l4, True),
        loads(4, rec, ww, False),
        loads(5, cot_r, mu, False),
    ]
    small = [
        pltpu.make_async_copy(a, b, small_sem.at[i])
        for i, (a, b) in enumerate(((sig_l_in, sig_l), (sig_t_in, sig_t), (region_in, region), (tissue_in, tissue)))
    ]
    for copy in small:
        copy.start()
    for group in copies:
        for copy in group:
            copy.start()

    barrier = pltpu.get_barrier_semaphore()

    def both(a, b):
        return jnp.logical_and(has[a], has[b])

    def target(*sides):
        return (gx + sum(step_of[s][0] for s in sides), gy + sum(step_of[s][1] for s in sides))

    for a, b in corner_list:

        @pl.when(both(a, b))
        def _(a=a, b=b):
            pl.semaphore_signal(barrier, inc=1, device_id=target(a, b), device_id_type=MESH)

    @pl.loop(1, gy_count)
    def _(k):
        pl.semaphore_signal(barrier, inc=1, device_id=(gx, lax.rem(gy + k, gy_count)), device_id_type=MESH)

    @pl.loop(1, gx_count)
    def _(k):
        pl.semaphore_signal(barrier, inc=1, device_id=(lax.rem(gx + k, gx_count), gy), device_id_type=MESH)

    gxi = (gx > 0).astype(jnp.int32) + (gx < gx_count - 1).astype(jnp.int32)
    gyi = (gy > 0).astype(jnp.int32) + (gy < gy_count - 1).astype(jnp.int32)

    def remote(src, dst, send, recv, device):
        return pltpu.make_async_remote_copy(
            src_ref=src, dst_ref=dst, send_sem=send, recv_sem=recv, device_id=device, device_id_type=MESH
        )

    zero = jnp.zeros((8, ZL), jnp.float32)
    face0 = jnp.zeros((2, NY, ZL), jnp.float32)
    line0 = jnp.zeros((1, ZL), jnp.float32)
    for f in fields:
        f[0, :, Y0 : Y0 + NY, :] = face0
        f[NX + 1, :, Y0 : Y0 + NY, :] = face0
    bb[0, :, Y0 : Y0 + NY, :] = face0

    @pl.loop(1, NX + 1)
    def _(p):
        for h in range(2):
            for f in fields:
                f[p, h, Y0 - 1 : Y0, :] = line0
                f[p, h, Y0 + NY : Y0 + NY + 1, :] = line0
            ay[p, h, Y0 - 1 : Y0, :] = line0
            py[p, h, Y0 + NY : Y0 + NY + 1, :] = line0

    for i, name in enumerate(names):

        @pl.when(jnp.logical_not(has[name]))
        def _(i=i):
            for k in range(8):
                halo[k, i, :, Y0 : Y0 + NY, :] = face0
            for c in range(3):
                frecv[i, c] = face0
            trecv[i] = zero

    for c, (a, b) in enumerate(corner_list):

        @pl.when(jnp.logical_not(both(a, b)))
        def _(c=c):
            for k in range(8):
                crecv[k, c] = jnp.zeros((2, 8, ZL), jnp.float32)

    for i in range(4):
        for h in range(2):
            cfo[i, 0, h, Y0 - 1 : Y0, :] = line0
            cfo[i, 0, h, Y0 + NY : Y0 + NY + 1, :] = line0
    acc[...] = jnp.zeros_like(acc)

    for copy in small:
        copy.wait()
    lanes = lane()
    tile_of = lanes // TILE

    def lane_vector(ref, h):
        value = zero
        for k in range(4):
            value = jnp.where(tile_of == k, ref[0, 0, 4 * h + k].astype(jnp.float32), value)
        return value

    own_r = [lane_vector(region, h) for h in range(2)]
    own_t = [lane_vector(tissue, h) for h in range(2)]
    sub = lax.broadcasted_iota(jnp.int32, (8, ZL), 0)
    subf = sub.astype(jnp.float32)
    tinfo[...] = jnp.where(
        sub == 0, own_r[0], jnp.where(sub == 1, own_r[1], jnp.where(sub == 2, own_t[0], own_t[1]))
    )
    value = jnp.where(
        lanes < 64, jnp.where(sub == 2 * gy, sig_l[0], sig_l[1]), jnp.where(sub == 2 * gy, sig_t[0], sig_t[1])
    )
    mine = jnp.where(jnp.logical_or(sub == 2 * gy, sub == 2 * gy + 1), value, 0.0)
    g1send[...] = mine

    other = (1, 0, 3, 2)

    def start(list_):
        for cond, _, copy in list_:

            @pl.when(cond)
            def _(copy=copy):
                copy.start()

    def wait_recv(list_):
        for _, cond, copy in list_:

            @pl.when(cond)
            def _(copy=copy):
                copy.wait_recv()

    def wait_send(list_):
        for cond, _, copy in list_:

            @pl.when(cond)
            def _(copy=copy):
                copy.wait_send()

    def to_faces(sources, dest, send, recv):
        return [
            (has[s], has[names[other[i]]], remote(sources[i], dest(other[i]), send(i), recv(other[i]), target(s)))
            for i, s in enumerate(names)
        ]

    def tile_copies():
        return to_faces([tinfo] * 4, lambda i: trecv.at[i], lambda i: ts.at[i], lambda i: tr.at[i])

    def fiber_exchange():
        first = pl.ds(0, 3)
        sources = [fp.at[first, 1, :, data, :], fp.at[first, NX, :, data, :], fysend.at[0], fysend.at[1]]
        return to_faces(sources, lambda i: frecv.at[i], lambda i: fs.at[i], lambda i: fr.at[i])

    def exchange(k):
        f = fields[k]
        sources = [f.at[1, :, data, :], f.at[NX, :, data, :], ysend.at[k, 0, :, data, :], ysend.at[k, 1, :, data, :]]
        out = to_faces(
            sources, lambda i: halo.at[k, i, :, data, :], lambda i: xs.at[k, i], lambda i: xr.at[k, i]
        )
        for c, (a, b) in enumerate(corner_list):
            xrow = Y0 if a == "l" else Y0 + NX - 8
            src = ysend.at[k, 0 if b == "d" else 1, :, pl.ds(xrow, 8), :]
            copy = remote(src, crecv.at[k, 3 - c], xs.at[k, 4 + c], xr.at[k, 7 - c], target(a, b))
            out.append((both(a, b), both(*corner_list[3 - c]), copy))
        return out

    def g1(k):
        return remote(g1send, g1recv.at[k], g1s.at[k], g1r.at[k], (gx, lax.rem(gy + k, gy_count)))

    def g2(k):
        return remote(quad.at[0], quad.at[k], g2s, g2r, (lax.rem(gx + k, gx_count), gy))

    def wait_load(index):
        for copy in copies[index]:
            copy.wait()

    def pack_rows(f, k):
        @pl.loop(0, NX)
        def _(x):
            for h in range(2):
                ysend[k, 0, h, pl.ds(x + Y0, 1), :] = f[x + 1, h, Y0 : Y0 + 1, :]
                ysend[k, 1, h, pl.ds(x + Y0, 1), :] = f[x + 1, h, Y0 + NY - 1 : Y0 + NY, :]

    def trig(x):
        for yt in range(YT):
            y = yt * 8
            for h in range(2):
                got = products(tt[x, h, y : y + 8, :], bb[x + 1, h, Y0 + y : Y0 + y + 8, :])
                for c in range(6):
                    fp[c, x + 1, h, Y0 + y : Y0 + y + 8, :] = got[c]
                for i, c in enumerate((YY, XY, YZ)):
                    if yt == 0:
                        fysend[0, i, h, pl.ds(x, 1), :] = got[c][0:1]
                    if yt == YT - 1:
                        fysend[1, i, h, pl.ds(x, 1), :] = got[c][7:8]

    wait_load(0)
    wait_load(1)
    pl.loop(0, NX // 2)(trig)
    pl.semaphore_wait(barrier, gx_count - 1 + gy_count - 1 + gxi * gyi)
    for k in range(1, gy_count):
        g1(k).start()
    start(tile_copies())
    wait_load(2)
    pack_rows(u0, 0)
    start(exchange(0))
    pl.loop(NX // 2, 3 * NX // 4)(trig)
    quad_own = mine
    for k in range(1, gy_count):
        g1(k).wait_recv()
        quad_own = quad_own + g1recv[k]
    quad[0] = quad_own

    @pl.loop(1, gx_count)
    def _(k):
        g2(k).start()

    pl.loop(3 * NX // 4, NX)(trig)
    start(fiber_exchange())
    wait_load(3)
    pack_rows(l4, 4)
    start(exchange(4))

    wait_recv(tile_copies())
    remote(quad.at[pl.ds(1, gx_count - 1)], quad.at[pl.ds(1, gx_count - 1)], g2s, g2r, (gx, gy)).wait_recv()
    regions = list(own_r)
    flags = list(own_t)
    for i in range(4):
        for h in range(2):
            regions.append(jnp.broadcast_to(trecv[i, h : h + 1, :], (8, ZL)))
            flags.append(jnp.broadcast_to(trecv[i, 2 + h : 3 + h, :], (8, ZL)))

    def lookup(k, sums):
        tile = quad[k]
        turned = pltpu.roll(tile, 64, 1)
        low = lanes < 64
        long_, trans = jnp.where(low, tile, turned), jnp.where(low, turned, tile)
        group = lax.rem(gx - k + gx_count, gx_count)
        ids = subf + (8 * group).astype(jnp.float32)
        new = []
        for i in range(10):
            hit = regions[i] == ids
            new.append(jnp.where(hit, long_, sums[2 * i]))
            new.append(jnp.where(hit, trans, sums[2 * i + 1]))
        return tuple(new)

    sums = lax.fori_loop(0, gx_count, lookup, (zero,) * 20)
    for i in range(10):
        s_l = jnp.broadcast_to(jnp.sum(sums[2 * i], axis=0, keepdims=True), (8, ZL)) * flags[i]
        s_t = jnp.broadcast_to(jnp.sum(sums[2 * i + 1], axis=0, keepdims=True), (8, ZL)) * flags[i]
        sv[i // 2, 0, i % 2] = s_t
        sv[i // 2, 1, i % 2] = s_l - s_t

    c_pair = 0.25 * DT
    c_axis = 0.5 * DT
    st = pair(lambda h: sv[0, 0, h])
    ee = pair(lambda h: sv[0, 1, h])
    ea = pair(lambda h: c_axis * ee[h])
    ep = pair(lambda h: c_pair * ee[h])
    s2 = pair(lambda h: DT * st[h])

    def coefficients(p):
        for yt in range(YT):
            y = yt * 8
            r = slice(Y0 + y, Y0 + y + 8)
            q = slice(y, y + 8)
            dzz = []
            for h in range(2):
                sum_x = fp[XX, p, h, r, :] + fp[XX, p + 1, h, r, :]
                sum_y = fp[YY, p, h, r, :] + fp[YY, p, h, Y0 + y + 1 : Y0 + y + 9, :]
                if yt == YT - 1:
                    sum_y = jnp.where(sub == 7, 0.0, sum_y)
                fhx[p, h, q, :] = sum_x
                fhy[p, h, q, :] = sum_y
                dx[p, h, q, :] = s2[h] + ea[h] * sum_x
                dy[p, h, q, :] = s2[h] + ea[h] * sum_y
                dzz.append(c_axis * st[h] + ea[h] * fp[ZZ, p, h, r, :])
                for i, c in enumerate((XY, XZ, YZ)):
                    ex[i, p, h, q, :] = ep[h] * fp[c, p, h, r, :]
            up = z_up(*dzz)
            for h in range(2):
                dz[p, h, q, :] = dzz[h] + up[h]
            dzm[p, q, :] = dzz[0]

    pl.loop(1, NX + 1)(coefficients)
    wait_recv(fiber_exchange())

    def own_products(i, c, h, t):
        if i < 2:
            return fp[(XX, XY, XZ)[c], 1 if i == 0 else NX, h, Y0 + t * 8 : Y0 + t * 8 + 8, :]
        return fysend[i - 2, c, h, t * 8 : t * 8 + 8, :]

    for i in range(4):
        for h in range(2):
            st_n, e_n = sv[1 + i, 0, h], sv[1 + i, 1, h]
            for t in range(4):
                q = slice(t * 8, t * 8 + 8)
                total = (st_n + e_n * frecv[i, 0, h, q, :]) + (st[h] + ee[h] * own_products(i, 0, h, t))
                cfd[i, h, q, :] = c_axis * total
                if i == 1:
                    dx[NX, h, q, :] = c_axis * total
                    fhx[NX, h, q, :] = zero
                for j in range(2):
                    cfh[i, j, h, q, :] = c_pair * e_n * frecv[i, 1 + j, h, q, :]
                    cfo[i, j, h, Y0 + t * 8 : Y0 + t * 8 + 8, :] = ep[h] * own_products(i, 1 + j, h, t)

    for x in range(NX):
        for h in range(2):
            dy[x + 1, h, NY - 1 : NY, :] = cfd[3, h, x : x + 1, :]

    def rows(y, shift=0):
        return slice(Y0 + y + shift, Y0 + y + shift + 8)

    def near(f, p, y):
        c = pair(lambda h: f[p, h, rows(y), :])
        xp = pair(lambda h: f[p + 1, h, rows(y), :])
        xm = pair(lambda h: f[p - 1, h, rows(y), :])
        yp = pair(lambda h: f[p, h, rows(y, 1), :])
        ym = pair(lambda h: f[p, h, rows(y, -1), :])
        return c, xp, xm, yp, ym, z_up(*c), z_down(*c)

    def stage_a(f, p, yt, react, sens=None):
        y = yt * 8
        q = slice(y, y + 8)
        c, xp, xm, yp, ym, zp, zm = near(f, p, y)
        own = react(p, y, c)
        if sens is not None:
            u, sums = sens
            v, vxp, vxm, vyp, vym, vzp, vzm = near(u, p, y)
        flux_x, local, pz, az, prod_z = [], [], [], [], []
        for h in range(2):
            g_x, g_y, g_z = xp[h] - xm[h], yp[h] - ym[h], zp[h] - zm[h]
            if sens is None:
                e_xy, e_xz, e_yz = (ex[i, p, h, q, :] for i in range(3))
            else:
                e_xy, e_xz, e_yz = (fp[i, p, h, rows(y), :] for i in (XY, XZ, YZ))
            p_x = e_xy * g_y + e_xz * g_z
            p_y = e_xy * g_x + e_yz * g_z
            p_z = e_xz * g_x + e_yz * g_y
            d_x, d_y, d_z = xp[h] - c[h], yp[h] - c[h], zp[h] - c[h]
            if sens is not None:
                cross = (vxp[h] - vxm[h]) * p_x + (vyp[h] - vym[h]) * p_y + (vzp[h] - vzm[h]) * p_z
                m_x, m_y, m_z = d_x * (vxp[h] - v[h]), d_y * (vyp[h] - v[h]), d_z * (vzp[h] - v[h])
                sums[h] = sums[h] + ((fhx[p, h, q, :] * m_x + fhy[p, h, q, :] * m_y) + 0.5 * cross)
                sums[2 + h] = sums[2 + h] + (m_x + m_y)
                prod_z.append(m_z)
                p_x, p_y, p_z = ep[h] * p_x, ep[h] * p_y, ep[h] * p_z
            f_x = dx[p, h, q, :] * d_x
            f_y = dy[p, h, q, :] * d_y
            f_z = dz[p, h, q, :] * d_z
            back = bb[p - 1, h, rows(y), :]
            bb[p, h, rows(y), :] = f_x + p_x
            py[p, h, rows(y), :] = p_y
            ay[p, h, rows(y), :] = f_y + p_y
            pz.append(p_z)
            az.append(f_z + p_z)
            flux_x.append(p_x)
            local.append((own[h] + f_x) + (f_y - back))
            local[h] = local[h] + f_z
        up = z_up(*pz)
        down = z_down(*az, edge=dzm[p, q, :] * c[0])
        for h in range(2):
            tt[p - 1, h, q, :] = local[h] + (up[h] - down[h])
        if sens is not None:
            below = z_down(*prod_z, edge=c[0] * v[0])
            for h in range(2):
                m = prod_z[h] + below[h]
                sums[h] = sums[h] + fp[ZZ, p, h, rows(y), :] * m
                sums[4 + h] = sums[4 + h] + m
        return flux_x

    def stage_b(p, yt, flux_x, put):
        y = yt * 8
        for h in range(2):
            value = tt[p - 1, h, y : y + 8, :] + (py[p, h, rows(y, 1), :] - ay[p, h, rows(y, -1), :])
            put(p, h, yt, value if flux_x is None else value + flux_x[h])

    def apply(k, react, put, u=None):
        f = fields[k]
        sums = [zero] * 6

        def stage(p, yt, running):
            return stage_a(f, p, yt, react, None if u is None else (u, running))

        for yt in range(YT):
            stage(1, yt, sums)

        def body(p, carry):
            running = list(carry)
            for yt in range(YT):
                stage_b(p - 1, yt, stage(p, yt, running), put)
            return tuple(running)

        if u is None:
            lax.fori_loop(2, NX + 1, lambda p, carry: (body(p, [zero] * 6), carry)[1], 0)
        else:
            sums = lax.fori_loop(2, NX + 1, body, tuple(sums))
            for h in range(2):
                acc[h] = acc[h] + sums[h]
                acc[2 + h] = acc[2 + h] + (2.0 * sums[2 + h] + sums[4 + h])
        for yt in range(YT):
            stage_b(NX, yt, None, put)

    def put_to(ref, slot, plane0, row0):
        def put(p, h, yt, value):
            ref[p - 1 + plane0, h, row0 + yt * 8 : row0 + yt * 8 + 8, :] = value
            if yt == 0:
                ysend[slot, 0, h, pl.ds(p - 1 + Y0, 1), :] = value[0:1]
            if yt == YT - 1:
                ysend[slot, 1, h, pl.ds(p - 1 + Y0, 1), :] = value[7:8]

        return put

    def install(k):
        for c, (a, b) in enumerate(corner_list):
            at = 7 if a == "l" else 0
            for h in range(2):
                v = crecv[k, c, h, at : at + 1, :]
                row = Y0 - 1 if b == "d" else Y0 + NY
                halo[k, names.index(a), h, row : row + 1, :] = v
                row = Y0 - 1 if a == "l" else Y0 + NX
                halo[k, names.index(b), h, row : row + 1, :] = v
        for s in range(2):
            row = Y0 if s == 0 else Y0 + NY - 1
            for h in range(2):
                ysend[k, s, h, Y0 - 1 : Y0, :] = halo[k, 0, h, row : row + 1, :]
                ysend[k, s, h, Y0 + NX : Y0 + NX + 1, :] = halo[k, 1, h, row : row + 1, :]

    def layer(k, i, h, r):
        if i < 2:
            return fields[k][1 if i == 0 else NX, h, r, :]
        return ysend[k, i - 2, h, r, :]

    def delta(k, i, t):
        lo = i in (0, 2)
        y = t * 8
        q = slice(y, y + 8)
        c = pair(lambda h: halo[k, i, h, rows(y), :])
        zp, zm = z_up(*c), z_down(*c)
        turn = pair(lambda h: cfo[i, 1, h, rows(y), :] * c[h])
        tp, tm = z_up(*turn), z_down(*turn)
        out = []
        for h in range(2):
            bp, bm = halo[k, i, h, rows(y, 1), :], halo[k, i, h, rows(y, -1), :]
            total = cfh[i, 0, h, q, :] * (bp - bm) + cfh[i, 1, h, q, :] * (zp[h] - zm[h])
            total = total + (cfo[i, 0, h, rows(y, 1), :] * bp - cfo[i, 0, h, rows(y, -1), :] * bm)
            total = total + (tp[h] - tm[h])
            if lo:
                out.append(cfd[i, h, q, :] * (c[h] - layer(k, i, h, rows(y))) - total)
            else:
                out.append(cfd[i, h, q, :] * c[h] + total)
        return out

    def finish(k, ref, slot, plane0, row0):
        wait_recv(exchange(k))
        install(k)
        for i, plane in ((0, plane0), (1, plane0 + NX - 1)):
            for t in range(4):
                d = delta(k, i, t)
                for h in range(2):
                    r = slice(row0 + t * 8, row0 + t * 8 + 8)
                    ref[plane, h, r, :] = ref[plane, h, r, :] + d[h]
            x = Y0 if i == 0 else Y0 + NX - 1
            for h in range(2):
                ysend[slot, 0, h, x : x + 1, :] = ref[plane, h, row0 : row0 + 1, :]
                ysend[slot, 1, h, x : x + 1, :] = ref[plane, h, row0 + NY - 1 : row0 + NY, :]
        for i in (2, 3):
            for t in range(4):
                d = delta(k, i, t)
                for h in range(2):
                    ysend[slot, i - 2, h, rows(t * 8), :] = ysend[slot, i - 2, h, rows(t * 8), :] + d[h]
        for x in (0, NX - 1):
            write_back(x, ref, slot, plane0, row0)

    def write_back(x, ref, slot, plane0, row0):
        for h in range(2):
            ref[x + plane0, h, row0 : row0 + 1, :] = ysend[slot, 0, h, x + Y0 : x + Y0 + 1, :]
            ref[x + plane0, h, row0 + NY - 1 : row0 + NY, :] = ysend[slot, 1, h, x + Y0 : x + Y0 + 1, :]

    def write_back_rest(ref, slot, plane0, row0):
        for x in range(1, NX - 1):
            write_back(x, ref, slot, plane0, row0)

    def store(ref, out, index):
        return [
            pltpu.make_async_copy(ref.at[:, h], out.at[:, :, pl.ds(h * ZL, ZL)], load_sem.at[index, h]) for h in range(2)
        ]

    wait_load(4)
    wait_load(5)
    for n in range(STEPS):

        def react(p, y, c, n=n):
            q = slice(y, y + 8)
            out = []
            for h in range(2):
                w = ww[p - 1, h, q, :]
                u = c[h]
                part = (8.0 * DT) * u
                turn = 8.0 * DT * 1.15 - part
                poly_ = u * turn
                rate = ((1.0 - 8.0 * DT * 0.15) - DT * w) + poly_
                out.append(u * rate)
                rs[n][p - 1, h, q, :] = rate + u * (turn - part)
                if n < STEPS - 1:
                    ww[p - 1, h, q, :] = (1.0 - DT * EPS_W) * w + EPS_W * poly_
            return out

        if n < STEPS - 1:
            place = (fields[n + 1], n + 1, 1, Y0)
        else:
            place = (ulast, 8, 0, 0)
        apply(n, react, put_to(*place))
        finish(n, *place)
        if n < STEPS - 1:
            start(exchange(n + 1))
        write_back_rest(*place)
    for copy in store(ulast, out_u, 0):
        copy.start()

    c_mu = 16.0 * DT * EPS_W

    def face_sums(n, k):
        sums = [zero] * 4
        for i in range(4):
            lo = i in (0, 2)
            for t in range(4):
                y = t * 8
                for_z = [pair(lambda h: layer(f, i, h, rows(y))) for f in (n, k)]
                zs = [(z_up(*c), z_down(*c)) for c in for_z]
                for h in range(2):
                    f_aa, f_ab, f_az = (own_products(i, c, h, t) for c in range(3))
                    flux = [
                        f_ab * (layer(f, i, h, rows(y, 1)) - layer(f, i, h, rows(y, -1))) + f_az * (z[0][h] - z[1][h])
                        for f, z in zip((n, k), zs)
                    ]
                    h_u, h_l = halo[n, i, h, rows(y), :], halo[k, i, h, rows(y), :]
                    o_u, o_l = for_z[0][h], for_z[1][h]
                    m = (o_u - h_u) * (o_l - h_l)
                    cross = 0.5 * (h_u * flux[1] + h_l * flux[0])
                    sums[h] = sums[h] + (f_aa * m - cross if lo else f_aa * m + cross)
                    sums[2 + h] = sums[2 + h] + (m if lo else m - 2.0 * (o_u * o_l))
        for i in range(4):
            acc[i] = acc[i] + sums[i]

    for n in range(STEPS - 1, -1, -1):
        k = 4 + STEPS - 1 - n

        def react(p, y, c, n=n):
            q = slice(y, y + 8)
            out = []
            for h in range(2):
                u = us[n][p, h, rows(y), :]
                m = mu[p - 1, h, q, :]
                if n == STEPS - 1:
                    m = c_mu * m
                out.append(c[h] * rs[n][p - 1, h, q, :] - (u - 0.575) * m)
                if n > 0:
                    mu[p - 1, h, q, :] = (1.0 - DT * EPS_W) * m - ((DT * c_mu) * c[h]) * u
            return out

        place = (fields[k + 1], k + 1, 1, Y0) if n > 0 else (llast, 9, 0, 0)
        apply(k, react, put_to(*place), us[n])
        finish(k, *place)
        if n > 0:
            start(exchange(k + 1))
        write_back_rest(*place)
        face_sums(n, k)
    for copy in store(llast, out_lam, 1):
        copy.start()

    scale = -0.5 * DT / TILE**1.5
    flat = []
    for h in range(2):
        s_l = jnp.broadcast_to(jnp.sum(acc[h], axis=0, keepdims=True), (8, ZL))
        s_a = jnp.broadcast_to(jnp.sum(acc[2 + h], axis=0, keepdims=True), (8, ZL))
        flat.append((scale * own_t[h] * s_l, scale * own_t[h] * (s_a - s_l)))

    def parts_of(group):
        ids = subf + (8 * group).astype(jnp.float32)
        tot = []
        for j in range(2):
            v = sum(jnp.where(own_r[h] == ids, flat[h][j], 0.0) for h in range(2))
            tot.append(v + pltpu.roll(v, 64, 1))
        return jnp.where(lanes < 64, tot[0], tot[1])

    rrecv[0] = parts_of(gx)

    def r1(k):
        return remote(rsend.at[k], rrecv.at[k], r1s, r1r, (lax.rem(gx + k, gx_count), gy))

    @pl.loop(1, gx_count)
    def _(k):
        rsend[k] = parts_of(lax.rem(gx + k, gx_count))
        r1(k).start()

    wait_send(tile_copies())
    wait_send(fiber_exchange())
    for k in range(8):
        wait_send(exchange(k))
    for k in range(1, gy_count):
        g1(k).wait_send()
    remote(quad.at[pl.ds(1, gx_count - 1)], quad.at[pl.ds(1, gx_count - 1)], g2s, g2r, (gx, gy)).wait_send()

    remote(rsend.at[pl.ds(1, gx_count - 1)], rrecv.at[pl.ds(1, gx_count - 1)], r1s, r1r, (gx, gy)).wait_recv()
    total = lax.fori_loop(0, gx_count, lambda k, s: s + rrecv[k], zero)
    rg[0] = total

    def r2(k):
        return remote(rg.at[0], rg.at[k], r2s.at[k], r2r.at[k], (gx, lax.rem(gy + k, gy_count)))

    for k in range(1, gy_count):
        r2(k).start()
    for k in range(1, gy_count):
        r2(k).wait_recv()
        total = total + rg[k]
    for j in range(2):
        mine_row = sub == 2 * gy + j
        out_l[j] = jnp.sum(jnp.where(jnp.logical_and(mine_row, lanes < 64), total, 0.0))
        out_t[j] = jnp.sum(jnp.where(jnp.logical_and(mine_row, lanes >= 64), total, 0.0))
    for k in range(1, gy_count):
        r2(k).wait_send()
    remote(rsend.at[pl.ds(1, gx_count - 1)], rrecv.at[pl.ds(1, gx_count - 1)], r1s, r1r, (gx, gy)).wait_send()
    for copy in store(ulast, out_u, 0) + store(llast, out_lam, 1):
        copy.wait()


def hand_on(u, lam, g_l, g_t, out_u, out_lam, out_l, out_t):
    out_u[...] = u[...]
    out_lam[...] = lam[...]
    for j in range(2):
        out_l[j] = g_l[j]
        out_t[j] = g_t[j]


def solution(mesh):
    gx_count, gy_count = mesh.shape["gx"], mesh.shape["gy"]

    def local(*args):
        any_, smem = pl.BlockSpec(memory_space=pl.ANY), pl.BlockSpec(memory_space=pltpu.SMEM)
        f32 = jnp.float32
        padded = pltpu.VMEM((NX + 2, 2, YP, ZL), f32)
        plain = pltpu.VMEM((NX, 2, NY, ZL), f32)
        dma = pltpu.SemaphoreType.DMA
        def vmem(*shape):
            return pltpu.VMEM(shape, f32)

        scratch = [padded] * 8 + [plain] * 2 + [plain] * 4 + [plain] * 2
        scratch += [
            vmem(6, NX + 2, 2, YP, ZL),
            vmem(NX + 1, 2, NY, ZL),
            vmem(NX + 1, 2, NY, ZL),
            vmem(NX + 1, 2, NY, ZL),
            vmem(NX + 1, NY, ZL),
            vmem(3, NX + 1, 2, NY, ZL),
            vmem(NX + 1, 2, NY, ZL),
            vmem(NX + 1, 2, NY, ZL),
            plain,
            padded,
            padded,
            padded,
            vmem(10, 2, 2, YP, ZL),
            vmem(8, 4, 2, YP, ZL),
            vmem(8, 4, 2, 8, ZL),
            vmem(2, 3, 2, NX, ZL),
            vmem(4, 3, 2, NX, ZL),
            vmem(4, 2, NX, ZL),
            vmem(4, 2, 2, NX, ZL),
            vmem(4, 2, 2, YP, ZL),
            vmem(8, ZL),
            vmem(4, 8, ZL),
            vmem(8, ZL),
            vmem(gy_count, 8, ZL),
            vmem(gx_count, 8, ZL),
            vmem(gx_count, 8, ZL),
            vmem(gx_count, 8, ZL),
            vmem(gy_count, 8, ZL),
            vmem(5, 2, 2, 8, ZL),
            vmem(4, 8, ZL),
            pltpu.SMEM((2,), f32),
            pltpu.SMEM((2,), f32),
            pltpu.SMEM((1, 1, 8), jnp.int32),
            pltpu.SMEM((1, 1, 8), jnp.int32),
            dma((6, 2)),
            dma((4,)),
            dma((8, 8)),
            dma((8, 8)),
            dma((4,)),
            dma((4,)),
            dma((4,)),
            dma((4,)),
            dma((gy_count,)),
            dma((gy_count,)),
            dma(()),
            dma(()),
            dma(()),
            dma(()),
            dma((gy_count,)),
            dma((gy_count,)),
        ]
        field = jax.ShapeDtypeStruct((NX, NY, 2 * ZL), f32)
        two = jax.ShapeDtypeStruct((2,), f32)

        def body(*refs):
            kernel(gx_count, gy_count, *refs)

        block = pl.BlockSpec((NX // 4, NY, 2 * ZL), lambda i: (i, 0, 0))
        made = pl.pallas_call(
            body,
            out_shape=(field, field, two, two),
            in_specs=[any_] * 9,
            out_specs=(any_, any_, smem, smem),
            scratch_shapes=scratch,
            compiler_params=pltpu.CompilerParams(
                collective_id=0, has_side_effects=True, vmem_limit_bytes=60 * 1024 * 1024
            ),
        )(*args[:3], *args[7:], *args[3:7])
        return pl.pallas_call(
            hand_on,
            grid=(4,),
            out_shape=(field, field, two, two),
            in_specs=[block, block, smem, smem],
            out_specs=(block, block, smem, smem),
        )(*made)

    return jax.shard_map(
        local,
        mesh=mesh,
        in_specs=(
            P("gx", "gy", None),
            P("gx", "gy", None),
            P(None, "gx", "gy", None),
            P(("gx", "gy")),
            P(("gx", "gy")),
            P("gx", "gy", None),
            P("gx", "gy", None),
            P("gx", "gy", None),
            P("gx", "gy", None),
        ),
        out_specs=(P("gx", "gy", None), P("gx", "gy", None), P(("gx", "gy")), P(("gx", "gy"))),
        check_vma=False,
    )
```

```python
import jax
import jax.numpy as jnp
from jax import lax
from jax.experimental import pallas as pl
from jax.experimental.pallas import tpu as pltpu
from jax.sharding import PartitionSpec as P

MESH = pl.DeviceIdType.MESH
STEPS = 4
DT = 0.05
EPS_W = 0.1
NX, NY, ZL = 32, 32, 128
Y0 = 8
YP = 48
YT = NY // 8
TILE = 32

XX, XY, XZ, YZ, YY, ZZ = range(6)

SIN = (0.9999999954376937, -0.16666657521871267, 0.008333039791882324, -0.0001980823258586027, 2.603293610558432e-06)
COS = (
    0.9999999997626233,
    -0.4999999931520218,
    0.041666634639589036,
    -0.0013888340619260778,
    2.4759088421126325e-05,
    -2.6032335044441285e-07,
)


def poly(z, coefs):
    total = coefs[-1] * z + coefs[-2]
    for value in coefs[-3::-1]:
        total = total * z + value
    return total


def sincos(x):
    t = (1.5707963705062866 - jnp.abs(x)) - 4.371139000186241e-08
    z = t * t
    cosine = t * poly(z, SIN)
    size = poly(z, COS)
    return jnp.where(x < 0.0, -size, size), cosine


def products(theta, phi):
    st, ct = sincos(theta)
    sp, cp = sincos(phi)
    fx, fy, fz = cp * ct, cp * st, sp
    return {XX: fx * fx, YY: fy * fy, ZZ: fz * fz, XY: fx * fy, XZ: fx * fz, YZ: fy * fz}


def lane():
    return lax.broadcasted_iota(jnp.int32, (8, ZL), 1)


def z_up(h0, h1):
    last = lane() == ZL - 1
    r0, r1 = pltpu.roll(h0, ZL - 1, 1), pltpu.roll(h1, ZL - 1, 1)
    return jnp.where(last, r1, r0), jnp.where(last, 0.0, r1)


def z_down(h0, h1, edge=0.0):
    first = lane() == 0
    r0, r1 = pltpu.roll(h0, 1, 1), pltpu.roll(h1, 1, 1)
    return jnp.where(first, edge, r0), jnp.where(first, r0, r1)


def pair(fn):
    return fn(0), fn(1)


def kernel(
    gx_count,
    gy_count,
    pot,
    rec,
    fib,
    cot_p,
    cot_r,
    sig_l_in,
    sig_t_in,
    region_in,
    tissue_in,
    ulast,
    llast,
    out_l,
    out_t,
    u0,
    u1,
    u2,
    u3,
    l4,
    l3,
    l2,
    l1,
    r0,
    r1_,
    r2_,
    r3,
    ww,
    mu,
    fp,
    dx,
    dy,
    dz,
    dzm,
    ex,
    fhx,
    fhy,
    tt,
    bb,
    py,
    ay,
    px,
    gzs,
    dzs,
    ysend,
    halo,
    crecv,
    fysend,
    frecv,
    cfd,
    cfh,
    cfo,
    tinfo,
    trecv,
    g1send,
    g1recv,
    quad,
    rsend,
    rrecv,
    rg,
    sv,
    acc,
    sig_l,
    sig_t,
    region,
    tissue,
    load_sem,
    small_sem,
    xs,
    xr,
    fs,
    fr,
    ts,
    tr,
    g1s,
    g1r,
    g2s,
    g2r,
    r1s,
    r1r,
    r2s,
    r2r,
):
    gx, gy = lax.axis_index("gx"), lax.axis_index("gy")
    has = {"l": gx > 0, "r": gx < gx_count - 1, "d": gy > 0, "u": gy < gy_count - 1}
    us = (u0, u1, u2, u3)
    ls = (l4, l3, l2, l1)
    rs = (r0, r1_, r2_, r3)
    fields = us + ls
    data = pl.ds(Y0, NY)
    names = "lrdu"
    corner_list = (("l", "d"), ("l", "u"), ("r", "d"), ("r", "u"))
    step_of = {"l": (-1, 0), "r": (1, 0), "d": (0, -1), "u": (0, 1)}

    def loads(index, src, dst, padded):
        out = []
        for h in range(2):
            s = src.at[:, :, pl.ds(h * ZL, ZL)]
            d = dst.at[pl.ds(1, NX), h, data, :] if padded else dst.at[:, h]
            out.append(pltpu.make_async_copy(s, d, load_sem.at[index, h]))
        return out

    copies = [
        loads(0, fib.at[0], tt, False),
        loads(1, fib.at[1], bb, True),
        loads(2, pot, u0, True),
        loads(3, cot_p, l4, True),
        loads(4, rec, ww, False),
        loads(5, cot_r, mu, False),
    ]
    small = [
        pltpu.make_async_copy(a, b, small_sem.at[i])
        for i, (a, b) in enumerate(((sig_l_in, sig_l), (sig_t_in, sig_t), (region_in, region), (tissue_in, tissue)))
    ]
    for copy in small:
        copy.start()
    for group in copies:
        for copy in group:
            copy.start()

    barrier = pltpu.get_barrier_semaphore()

    def both(a, b):
        return jnp.logical_and(has[a], has[b])

    def target(*sides):
        return (gx + sum(step_of[s][0] for s in sides), gy + sum(step_of[s][1] for s in sides))

    for a, b in corner_list:

        @pl.when(both(a, b))
        def _(a=a, b=b):
            pl.semaphore_signal(barrier, inc=1, device_id=target(a, b), device_id_type=MESH)

    @pl.loop(1, gy_count)
    def _(k):
        pl.semaphore_signal(barrier, inc=1, device_id=(gx, lax.rem(gy + k, gy_count)), device_id_type=MESH)

    @pl.loop(1, gx_count)
    def _(k):
        pl.semaphore_signal(barrier, inc=1, device_id=(lax.rem(gx + k, gx_count), gy), device_id_type=MESH)

    gxi = (gx > 0).astype(jnp.int32) + (gx < gx_count - 1).astype(jnp.int32)
    gyi = (gy > 0).astype(jnp.int32) + (gy < gy_count - 1).astype(jnp.int32)

    def remote(src, dst, send, recv, device):
        return pltpu.make_async_remote_copy(
            src_ref=src, dst_ref=dst, send_sem=send, recv_sem=recv, device_id=device, device_id_type=MESH
        )

    zero = jnp.zeros((8, ZL), jnp.float32)
    face0 = jnp.zeros((2, NY, ZL), jnp.float32)
    line0 = jnp.zeros((1, ZL), jnp.float32)
    for f in fields:
        f[0, :, Y0 : Y0 + NY, :] = face0
        f[NX + 1, :, Y0 : Y0 + NY, :] = face0
    bb[0, :, Y0 : Y0 + NY, :] = face0

    @pl.loop(1, NX + 1)
    def _(p):
        for h in range(2):
            for f in fields:
                f[p, h, Y0 - 1 : Y0, :] = line0
                f[p, h, Y0 + NY : Y0 + NY + 1, :] = line0
            ay[p, h, Y0 - 1 : Y0, :] = line0
            py[p, h, Y0 + NY : Y0 + NY + 1, :] = line0

    for i, name in enumerate(names):

        @pl.when(jnp.logical_not(has[name]))
        def _(i=i):
            for k in range(8):
                halo[k, i, :, Y0 : Y0 + NY, :] = face0
            for c in range(3):
                frecv[i, c] = face0
            trecv[i] = zero

    for c, (a, b) in enumerate(corner_list):

        @pl.when(jnp.logical_not(both(a, b)))
        def _(c=c):
            for k in range(8):
                crecv[k, c] = jnp.zeros((2, 8, ZL), jnp.float32)

    for i in range(4):
        for h in range(2):
            cfo[i, 0, h, Y0 - 1 : Y0, :] = line0
            cfo[i, 0, h, Y0 + NY : Y0 + NY + 1, :] = line0
    acc[...] = jnp.zeros_like(acc)

    for copy in small:
        copy.wait()
    lanes = lane()
    tile_of = lanes // TILE

    def lane_vector(ref, h):
        value = zero
        for k in range(4):
            value = jnp.where(tile_of == k, ref[0, 0, 4 * h + k].astype(jnp.float32), value)
        return value

    own_r = [lane_vector(region, h) for h in range(2)]
    own_t = [lane_vector(tissue, h) for h in range(2)]
    sub = lax.broadcasted_iota(jnp.int32, (8, ZL), 0)
    subf = sub.astype(jnp.float32)
    tinfo[...] = jnp.where(
        sub == 0, own_r[0], jnp.where(sub == 1, own_r[1], jnp.where(sub == 2, own_t[0], own_t[1]))
    )
    value = jnp.where(
        lanes < 64, jnp.where(sub == 2 * gy, sig_l[0], sig_l[1]), jnp.where(sub == 2 * gy, sig_t[0], sig_t[1])
    )
    mine = jnp.where(jnp.logical_or(sub == 2 * gy, sub == 2 * gy + 1), value, 0.0)
    g1send[...] = mine

    other = (1, 0, 3, 2)

    def start(list_):
        for cond, _, copy in list_:

            @pl.when(cond)
            def _(copy=copy):
                copy.start()

    def wait_recv(list_):
        for _, cond, copy in list_:

            @pl.when(cond)
            def _(copy=copy):
                copy.wait_recv()

    def wait_send(list_):
        for cond, _, copy in list_:

            @pl.when(cond)
            def _(copy=copy):
                copy.wait_send()

    def to_faces(sources, dest, send, recv):
        return [
            (has[s], has[names[other[i]]], remote(sources[i], dest(other[i]), send(i), recv(other[i]), target(s)))
            for i, s in enumerate(names)
        ]

    def tile_copies():
        return to_faces([tinfo] * 4, lambda i: trecv.at[i], lambda i: ts.at[i], lambda i: tr.at[i])

    def fiber_exchange():
        first = pl.ds(0, 3)
        sources = [fp.at[first, 1, :, data, :], fp.at[first, NX, :, data, :], fysend.at[0], fysend.at[1]]
        return to_faces(sources, lambda i: frecv.at[i], lambda i: fs.at[i], lambda i: fr.at[i])

    def exchange(k):
        f = fields[k]
        sources = [f.at[1, :, data, :], f.at[NX, :, data, :], ysend.at[k, 0, :, data, :], ysend.at[k, 1, :, data, :]]
        out = to_faces(
            sources, lambda i: halo.at[k, i, :, data, :], lambda i: xs.at[k, i], lambda i: xr.at[k, i]
        )
        for c, (a, b) in enumerate(corner_list):
            xrow = Y0 if a == "l" else Y0 + NX - 8
            src = ysend.at[k, 0 if b == "d" else 1, :, pl.ds(xrow, 8), :]
            copy = remote(src, crecv.at[k, 3 - c], xs.at[k, 4 + c], xr.at[k, 7 - c], target(a, b))
            out.append((both(a, b), both(*corner_list[3 - c]), copy))
        return out

    def g1(k):
        return remote(g1send, g1recv.at[k], g1s.at[k], g1r.at[k], (gx, lax.rem(gy + k, gy_count)))

    def g2(k):
        return remote(quad.at[0], quad.at[k], g2s, g2r, (lax.rem(gx + k, gx_count), gy))

    def wait_load(index):
        for copy in copies[index]:
            copy.wait()

    def pack_rows(f, k):
        @pl.loop(0, NX)
        def _(x):
            for h in range(2):
                ysend[k, 0, h, pl.ds(x + Y0, 1), :] = f[x + 1, h, Y0 : Y0 + 1, :]
                ysend[k, 1, h, pl.ds(x + Y0, 1), :] = f[x + 1, h, Y0 + NY - 1 : Y0 + NY, :]

    def trig(x):
        for yt in range(YT):
            y = yt * 8
            for h in range(2):
                got = products(tt[x, h, y : y + 8, :], bb[x + 1, h, Y0 + y : Y0 + y + 8, :])
                for c in range(6):
                    fp[c, x + 1, h, Y0 + y : Y0 + y + 8, :] = got[c]
                for i, c in enumerate((YY, XY, YZ)):
                    if yt == 0:
                        fysend[0, i, h, pl.ds(x, 1), :] = got[c][0:1]
                    if yt == YT - 1:
                        fysend[1, i, h, pl.ds(x, 1), :] = got[c][7:8]

    wait_load(0)
    wait_load(1)
    pl.loop(0, 2)(lambda i: trig(i * (NX - 1)))
    pl.loop(1, 8)(trig)
    pl.semaphore_wait(barrier, gx_count - 1 + gy_count - 1 + gxi * gyi)
    for k in range(1, gy_count):
        g1(k).start()
    start(tile_copies())
    start(fiber_exchange()[:2])
    pl.loop(8, 20)(trig)
    quad_own = mine
    for k in range(1, gy_count):
        g1(k).wait_recv()
        quad_own = quad_own + g1recv[k]
    quad[0] = quad_own

    @pl.loop(1, gx_count)
    def _(k):
        g2(k).start()

    pl.loop(20, NX - 1)(trig)
    start(fiber_exchange()[2:])
    wait_load(2)
    pack_rows(u0, 0)
    start(exchange(0))
    wait_load(3)
    pack_rows(l4, 4)

    wait_recv(tile_copies())
    remote(quad.at[pl.ds(1, gx_count - 1)], quad.at[pl.ds(1, gx_count - 1)], g2s, g2r, (gx, gy)).wait_recv()
    regions = list(own_r)
    flags = list(own_t)
    for i in range(4):
        for h in range(2):
            regions.append(jnp.broadcast_to(trecv[i, h : h + 1, :], (8, ZL)))
            flags.append(jnp.broadcast_to(trecv[i, 2 + h : 3 + h, :], (8, ZL)))

    def lookup(k, sums):
        tile = quad[k]
        turned = pltpu.roll(tile, 64, 1)
        low = lanes < 64
        long_, trans = jnp.where(low, tile, turned), jnp.where(low, turned, tile)
        group = lax.rem(gx - k + gx_count, gx_count)
        ids = subf + (8 * group).astype(jnp.float32)
        new = []
        for i in range(10):
            hit = regions[i] == ids
            new.append(jnp.where(hit, long_, sums[2 * i]))
            new.append(jnp.where(hit, trans, sums[2 * i + 1]))
        return tuple(new)

    sums = lax.fori_loop(0, gx_count, lookup, (zero,) * 20)
    for i in range(10):
        s_l = jnp.broadcast_to(jnp.sum(sums[2 * i], axis=0, keepdims=True), (8, ZL)) * flags[i]
        s_t = jnp.broadcast_to(jnp.sum(sums[2 * i + 1], axis=0, keepdims=True), (8, ZL)) * flags[i]
        sv[i // 2, 0, i % 2] = s_t
        sv[i // 2, 1, i % 2] = s_l - s_t

    c_pair = 0.25 * DT
    c_axis = 0.5 * DT
    st = pair(lambda h: sv[0, 0, h])
    ee = pair(lambda h: sv[0, 1, h])
    ea = pair(lambda h: c_axis * ee[h])
    ep = pair(lambda h: c_pair * ee[h])
    s2 = pair(lambda h: DT * st[h])

    def coefficients(p):
        for yt in range(YT):
            y = yt * 8
            r = slice(Y0 + y, Y0 + y + 8)
            q = slice(y, y + 8)
            dzz = []
            for h in range(2):
                sum_x = fp[XX, p, h, r, :] + fp[XX, p + 1, h, r, :]
                sum_y = fp[YY, p, h, r, :] + fp[YY, p, h, Y0 + y + 1 : Y0 + y + 9, :]
                if yt == YT - 1:
                    sum_y = jnp.where(sub == 7, 0.0, sum_y)
                fhx[p, h, q, :] = sum_x
                fhy[p, h, q, :] = sum_y
                dx[p, h, q, :] = s2[h] + ea[h] * sum_x
                dy[p, h, q, :] = s2[h] + ea[h] * sum_y
                dzz.append(c_axis * st[h] + ea[h] * fp[ZZ, p, h, r, :])
                for i, c in enumerate((XY, XZ, YZ)):
                    ex[i, p, h, q, :] = ep[h] * fp[c, p, h, r, :]
            up = z_up(*dzz)
            for h in range(2):
                dz[p, h, q, :] = dzz[h] + up[h]
            dzm[p, q, :] = dzz[0]
            above = z_up(*pair(lambda h: fp[ZZ, p, h, r, :]))
            for h in range(2):
                fp[YY, p, h, r, :] = above[h]

    pl.loop(1, NX + 1)(coefficients)
    wait_recv(fiber_exchange())

    def own_products(i, c, h, t):
        if i < 2:
            return fp[(XX, XY, XZ)[c], 1 if i == 0 else NX, h, Y0 + t * 8 : Y0 + t * 8 + 8, :]
        return fysend[i - 2, c, h, t * 8 : t * 8 + 8, :]

    for i in range(4):
        for h in range(2):
            st_n, e_n = sv[1 + i, 0, h], sv[1 + i, 1, h]
            for t in range(4):
                q = slice(t * 8, t * 8 + 8)
                total = (st_n + e_n * frecv[i, 0, h, q, :]) + (st[h] + ee[h] * own_products(i, 0, h, t))
                cfd[i, h, q, :] = c_axis * total
                if i == 1:
                    dx[NX, h, q, :] = c_axis * total
                    fhx[NX, h, q, :] = zero
                for j in range(2):
                    cfh[i, j, h, q, :] = c_pair * e_n * frecv[i, 1 + j, h, q, :]
                    cfo[i, j, h, Y0 + t * 8 : Y0 + t * 8 + 8, :] = ep[h] * own_products(i, 1 + j, h, t)

    for x in range(NX):
        for h in range(2):
            dy[x + 1, h, NY - 1 : NY, :] = cfd[3, h, x : x + 1, :]

    def rows(y, shift=0):
        return slice(Y0 + y + shift, Y0 + y + shift + 8)

    def near(f, p, y, along_z=True):
        c = pair(lambda h: f[p, h, rows(y), :])
        xp = pair(lambda h: f[p + 1, h, rows(y), :])
        xm = pair(lambda h: f[p - 1, h, rows(y), :])
        yp = pair(lambda h: f[p, h, rows(y, 1), :])
        ym = pair(lambda h: f[p, h, rows(y, -1), :])
        around = (c, xp, xm, yp, ym)
        return (*around, z_up(*c), z_down(*c)) if along_z else around

    def stage_a(f, p, yt, react, backs, n, sens=None):
        y = yt * 8
        q = slice(y, y + 8)
        c, xp, xm, yp, ym, zp, zm = near(f, p, y)
        own = react(p, y, c)
        if sens is not None:
            u, sums = sens
            v, vxp, vxm, vyp, vym = near(u, p, y, False)
        local, pz, az = [], [], []
        for h in range(2):
            g_x, g_y, g_z = xp[h] - xm[h], yp[h] - ym[h], zp[h] - zm[h]
            if sens is None:
                e_xy, e_xz, e_yz = (ex[i, p, h, q, :] for i in range(3))
            else:
                e_xy, e_xz, e_yz = (fp[i, p, h, rows(y), :] for i in (XY, XZ, YZ))
            p_x = e_xy * g_y + e_xz * g_z
            p_y = e_xy * g_x + e_yz * g_z
            p_z = e_xz * g_x + e_yz * g_y
            d_x, d_y, d_z = xp[h] - c[h], yp[h] - c[h], zp[h] - c[h]
            if sens is None:
                gzs[n, p - 1, h, q, :] = g_z
                dzs[n, p - 1, h, q, :] = d_z
            else:
                cross = (vxp[h] - vxm[h]) * p_x + (vyp[h] - vym[h]) * p_y + gzs[n, p - 1, h, q, :] * p_z
                m_x, m_y, m_z = d_x * (vxp[h] - v[h]), d_y * (vyp[h] - v[h]), d_z * dzs[n, p - 1, h, q, :]
                sums[h] = sums[h] + (
                    (fhx[p, h, q, :] * m_x + fhy[p, h, q, :] * m_y) + (fp[ZZ, p, h, rows(y), :] * m_z + 0.5 * cross)
                )
                sums[2 + h] = sums[2 + h] + (m_x + m_y)
                sums[4 + h] = sums[4 + h] + m_z
                sums[6 + h] = sums[6 + h] + fp[YY, p, h, rows(y), :] * m_z
                if h == 0:
                    m_0 = c[0] * v[0]
                    sums[8] = sums[8] + fp[ZZ, p, 0, rows(y), :] * m_0
                    sums[9] = sums[9] + m_0
                p_x, p_y, p_z = ep[h] * p_x, ep[h] * p_y, ep[h] * p_z
            f_x = dx[p, h, q, :] * d_x
            f_y = dy[p, h, q, :] * d_y
            f_z = dz[p, h, q, :] * d_z
            back = backs[yt][h]
            bb[p, h, rows(y), :] = f_x + p_x
            py[p, h, rows(y), :] = p_y
            ay[p, h, rows(y), :] = f_y + p_y
            pz.append(p_z)
            az.append(f_z + p_z)
            px[p, h, q, :] = p_x
            local.append((own[h] + f_x) + (f_y - back))
            local[h] = local[h] + f_z
        up = z_up(*pz)
        down = z_down(*az, edge=dzm[p, q, :] * c[0])
        for h in range(2):
            tt[p - 1, h, q, :] = local[h] + (up[h] - down[h])

    def stage_b(p, yt, put, last=False):
        y = yt * 8
        for h in range(2):
            value = tt[p - 1, h, y : y + 8, :] + (py[p, h, rows(y, 1), :] - ay[p, h, rows(y, -1), :])
            put(p, h, yt, value if last else value + px[p + 1, h, y : y + 8, :])

    def apply(k, n, react, put, u=None):
        f = fields[k]

        def plane(p, running):
            backs = [pair(lambda h: bb[p - 1, h, rows(yt * 8), :]) for yt in range(YT)]
            for yt in range(YT):
                stage_a(f, p, yt, react, backs, n, None if u is None else (u, running))

        def body(p, carry, complete=True):
            running = list(carry)
            if complete:
                for yt in range(YT):
                    stage_b(p - 2, yt, put)
            plane(p, running)
            return tuple(running)

        sums = (zero,) * (0 if u is None else 10)
        sums = lax.fori_loop(1, 3, lambda p, carry: body(p, carry, False), sums)
        sums = lax.fori_loop(3, NX + 1, body, sums)
        if u is not None:
            over_l = z_down(sums[6], sums[7], edge=sums[8])
            over_t = z_down(sums[4], sums[5], edge=sums[9])
            for h in range(2):
                acc[h] = acc[h] + (sums[h] + over_l[h])
                acc[2 + h] = acc[2 + h] + (2.0 * sums[2 + h] + (sums[4 + h] + over_t[h]))
        for yt in range(YT):
            stage_b(NX - 1, yt, put)
        for yt in range(YT):
            stage_b(NX, yt, put, True)

    def put_to(ref, slot, plane0, row0):
        def put(p, h, yt, value):
            ref[p - 1 + plane0, h, row0 + yt * 8 : row0 + yt * 8 + 8, :] = value
            if yt == 0:
                ysend[slot, 0, h, pl.ds(p - 1 + Y0, 1), :] = value[0:1]
            if yt == YT - 1:
                ysend[slot, 1, h, pl.ds(p - 1 + Y0, 1), :] = value[7:8]

        return put

    def install(k):
        for c, (a, b) in enumerate(corner_list):
            at = 7 if a == "l" else 0
            for h in range(2):
                v = crecv[k, c, h, at : at + 1, :]
                row = Y0 - 1 if b == "d" else Y0 + NY
                halo[k, names.index(a), h, row : row + 1, :] = v
                row = Y0 - 1 if a == "l" else Y0 + NX
                halo[k, names.index(b), h, row : row + 1, :] = v
        for s in range(2):
            row = Y0 if s == 0 else Y0 + NY - 1
            for h in range(2):
                ysend[k, s, h, Y0 - 1 : Y0, :] = halo[k, 0, h, row : row + 1, :]
                ysend[k, s, h, Y0 + NX : Y0 + NX + 1, :] = halo[k, 1, h, row : row + 1, :]

    def layer(k, i, h, r):
        if i < 2:
            return fields[k][1 if i == 0 else NX, h, r, :]
        return ysend[k, i - 2, h, r, :]

    def delta(k, i, t):
        lo = i in (0, 2)
        y = t * 8
        q = slice(y, y + 8)
        c = pair(lambda h: halo[k, i, h, rows(y), :])
        zp, zm = z_up(*c), z_down(*c)
        turn = pair(lambda h: cfo[i, 1, h, rows(y), :] * c[h])
        tp, tm = z_up(*turn), z_down(*turn)
        out = []
        for h in range(2):
            bp, bm = halo[k, i, h, rows(y, 1), :], halo[k, i, h, rows(y, -1), :]
            total = cfh[i, 0, h, q, :] * (bp - bm) + cfh[i, 1, h, q, :] * (zp[h] - zm[h])
            total = total + (cfo[i, 0, h, rows(y, 1), :] * bp - cfo[i, 0, h, rows(y, -1), :] * bm)
            total = total + (tp[h] - tm[h])
            if lo:
                out.append(cfd[i, h, q, :] * (c[h] - layer(k, i, h, rows(y))) - total)
            else:
                out.append(cfd[i, h, q, :] * c[h] + total)
        return out

    def finish(k, ref, slot, plane0, row0, between=None):
        wait_recv(exchange(k))
        install(k)
        if between is not None:
            between()
        for i, plane in ((0, plane0), (1, plane0 + NX - 1)):
            for t in range(4):
                d = delta(k, i, t)
                for h in range(2):
                    r = slice(row0 + t * 8, row0 + t * 8 + 8)
                    ref[plane, h, r, :] = ref[plane, h, r, :] + d[h]
            x = Y0 if i == 0 else Y0 + NX - 1
            for h in range(2):
                ysend[slot, 0, h, x : x + 1, :] = ref[plane, h, row0 : row0 + 1, :]
                ysend[slot, 1, h, x : x + 1, :] = ref[plane, h, row0 + NY - 1 : row0 + NY, :]
        for i in (2, 3):
            for t in range(4):
                d = delta(k, i, t)
                for h in range(2):
                    ysend[slot, i - 2, h, rows(t * 8), :] = ysend[slot, i - 2, h, rows(t * 8), :] + d[h]
        for x in (0, NX - 1):
            write_back(x, ref, slot, plane0, row0)

    def write_back(x, ref, slot, plane0, row0):
        for h in range(2):
            ref[x + plane0, h, row0 : row0 + 1, :] = ysend[slot, 0, h, x + Y0 : x + Y0 + 1, :]
            ref[x + plane0, h, row0 + NY - 1 : row0 + NY, :] = ysend[slot, 1, h, x + Y0 : x + Y0 + 1, :]

    def write_back_rest(ref, slot, plane0, row0):
        for x in range(1, NX - 1):
            write_back(x, ref, slot, plane0, row0)

    wait_load(4)
    wait_load(5)
    for n in range(STEPS):

        def react(p, y, c, n=n):
            q = slice(y, y + 8)
            out = []
            for h in range(2):
                w = ww[p - 1, h, q, :]
                u = c[h]
                part = (8.0 * DT) * u
                turn = 8.0 * DT * 1.15 - part
                poly_ = u * turn
                rate = ((1.0 - 8.0 * DT * 0.15) - DT * w) + poly_
                out.append(u * rate)
                rs[n][p - 1, h, q, :] = rate + u * (turn - part)
                if n < STEPS - 1:
                    ww[p - 1, h, q, :] = (1.0 - DT * EPS_W) * w + EPS_W * poly_
            return out

        if n < STEPS - 1:
            place = (fields[n + 1], n + 1, 1, Y0)
        else:
            place = (ulast, 8, 0, 0)
        apply(n, n, react, put_to(*place))
        finish(n, *place)
        if n < STEPS - 1:
            start(exchange(n + 1))
        if n == 0:
            start(exchange(4))
        write_back_rest(*place)

    c_mu = 16.0 * DT * EPS_W

    def face_sums(n, k):
        sums = [zero] * 4
        for i in range(4):
            lo = i in (0, 2)
            for t in range(4):
                y = t * 8
                for_z = [pair(lambda h: layer(f, i, h, rows(y))) for f in (n, k)]
                zs = [(z_up(*c), z_down(*c)) for c in for_z]
                for h in range(2):
                    f_aa, f_ab, f_az = (own_products(i, c, h, t) for c in range(3))
                    flux = [
                        f_ab * (layer(f, i, h, rows(y, 1)) - layer(f, i, h, rows(y, -1))) + f_az * (z[0][h] - z[1][h])
                        for f, z in zip((n, k), zs)
                    ]
                    h_u, h_l = halo[n, i, h, rows(y), :], halo[k, i, h, rows(y), :]
                    o_u, o_l = for_z[0][h], for_z[1][h]
                    m = (o_u - h_u) * (o_l - h_l)
                    cross = 0.5 * (h_u * flux[1] + h_l * flux[0])
                    sums[h] = sums[h] + (f_aa * m - cross if lo else f_aa * m + cross)
                    sums[2 + h] = sums[2 + h] + (m if lo else m - 2.0 * (o_u * o_l))
        for i in range(4):
            acc[i] = acc[i] + sums[i]

    def r1(k):
        return remote(rsend.at[k], rrecv.at[k], r1s, r1r, (lax.rem(gx + k, gx_count), gy))

    def send_sums():
        scale = -0.5 * DT / TILE**1.5
        flat = []
        for h in range(2):
            s_l = jnp.broadcast_to(jnp.sum(acc[h], axis=0, keepdims=True), (8, ZL))
            s_a = jnp.broadcast_to(jnp.sum(acc[2 + h], axis=0, keepdims=True), (8, ZL))
            flat.append((scale * own_t[h] * s_l, scale * own_t[h] * (s_a - s_l)))

        def parts_of(group):
            ids = subf + (8 * group).astype(jnp.float32)
            tot = []
            for j in range(2):
                v = sum(jnp.where(own_r[h] == ids, flat[h][j], 0.0) for h in range(2))
                tot.append(v + pltpu.roll(v, 64, 1))
            return jnp.where(lanes < 64, tot[0], tot[1])

        rrecv[0] = parts_of(gx)

        @pl.loop(1, gx_count)
        def _(k):
            rsend[k] = parts_of(lax.rem(gx + k, gx_count))
            r1(k).start()

    for n in range(STEPS - 1, -1, -1):
        k = 4 + STEPS - 1 - n

        def react(p, y, c, n=n):
            q = slice(y, y + 8)
            out = []
            for h in range(2):
                u = us[n][p, h, rows(y), :]
                m = mu[p - 1, h, q, :]
                if n == STEPS - 1:
                    m = c_mu * m
                out.append(c[h] * rs[n][p - 1, h, q, :] - (u - 0.575) * m)
                if n > 0:
                    mu[p - 1, h, q, :] = (1.0 - DT * EPS_W) * m - ((DT * c_mu) * c[h]) * u
            return out

        place = (fields[k + 1], k + 1, 1, Y0) if n > 0 else (llast, 9, 0, 0)
        apply(k, n, react, put_to(*place), us[n])
        if n > 0:
            finish(k, *place)
            start(exchange(k + 1))
            write_back_rest(*place)
            face_sums(n, k)
        else:

            def between():
                face_sums(0, 7)
                send_sums()

            finish(k, *place, between)
            write_back_rest(*place)

    wait_send(tile_copies())
    wait_send(fiber_exchange())
    for k in range(8):
        wait_send(exchange(k))
    for k in range(1, gy_count):
        g1(k).wait_send()
    remote(quad.at[pl.ds(1, gx_count - 1)], quad.at[pl.ds(1, gx_count - 1)], g2s, g2r, (gx, gy)).wait_send()

    remote(rsend.at[pl.ds(1, gx_count - 1)], rrecv.at[pl.ds(1, gx_count - 1)], r1s, r1r, (gx, gy)).wait_recv()
    total = lax.fori_loop(0, gx_count, lambda k, s: s + rrecv[k], zero)
    rg[0] = total

    def r2(k):
        return remote(rg.at[0], rg.at[k], r2s.at[k], r2r.at[k], (gx, lax.rem(gy + k, gy_count)))

    for k in range(1, gy_count):
        r2(k).start()
    for k in range(1, gy_count):
        r2(k).wait_recv()
        total = total + rg[k]
    for j in range(2):
        mine_row = sub == 2 * gy + j
        out_l[j] = jnp.sum(jnp.where(jnp.logical_and(mine_row, lanes < 64), total, 0.0))
        out_t[j] = jnp.sum(jnp.where(jnp.logical_and(mine_row, lanes >= 64), total, 0.0))
    for k in range(1, gy_count):
        r2(k).wait_send()
    remote(rsend.at[pl.ds(1, gx_count - 1)], rrecv.at[pl.ds(1, gx_count - 1)], r1s, r1r, (gx, gy)).wait_send()


def solution(mesh):
    gx_count, gy_count = mesh.shape["gx"], mesh.shape["gy"]

    def local(*args):
        any_, smem = pl.BlockSpec(memory_space=pl.ANY), pl.BlockSpec(memory_space=pltpu.SMEM)
        f32 = jnp.float32
        padded = pltpu.VMEM((NX + 2, 2, YP, ZL), f32)
        plain = pltpu.VMEM((NX, 2, NY, ZL), f32)
        dma = pltpu.SemaphoreType.DMA
        def vmem(*shape):
            return pltpu.VMEM(shape, f32)

        scratch = [padded] * 8 + [plain] * 4 + [plain] * 2
        scratch += [
            vmem(6, NX + 2, 2, YP, ZL),
            vmem(NX + 1, 2, NY, ZL),
            vmem(NX + 1, 2, NY, ZL),
            vmem(NX + 1, 2, NY, ZL),
            vmem(NX + 1, NY, ZL),
            vmem(3, NX + 1, 2, NY, ZL),
            vmem(NX + 1, 2, NY, ZL),
            vmem(NX + 1, 2, NY, ZL),
            plain,
            padded,
            padded,
            padded,
            vmem(NX + 1, 2, NY, ZL),
            vmem(STEPS, NX, 2, NY, ZL),
            vmem(STEPS, NX, 2, NY, ZL),
            vmem(10, 2, 2, YP, ZL),
            vmem(8, 4, 2, YP, ZL),
            vmem(8, 4, 2, 8, ZL),
            vmem(2, 3, 2, NX, ZL),
            vmem(4, 3, 2, NX, ZL),
            vmem(4, 2, NX, ZL),
            vmem(4, 2, 2, NX, ZL),
            vmem(4, 2, 2, YP, ZL),
            vmem(8, ZL),
            vmem(4, 8, ZL),
            vmem(8, ZL),
            vmem(gy_count, 8, ZL),
            vmem(gx_count, 8, ZL),
            vmem(gx_count, 8, ZL),
            vmem(gx_count, 8, ZL),
            vmem(gy_count, 8, ZL),
            vmem(5, 2, 2, 8, ZL),
            vmem(4, 8, ZL),
            pltpu.SMEM((2,), f32),
            pltpu.SMEM((2,), f32),
            pltpu.SMEM((1, 1, 8), jnp.int32),
            pltpu.SMEM((1, 1, 8), jnp.int32),
            dma((6, 2)),
            dma((4,)),
            dma((8, 8)),
            dma((8, 8)),
            dma((4,)),
            dma((4,)),
            dma((4,)),
            dma((4,)),
            dma((gy_count,)),
            dma((gy_count,)),
            dma(()),
            dma(()),
            dma(()),
            dma(()),
            dma((gy_count,)),
            dma((gy_count,)),
        ]
        field = jax.ShapeDtypeStruct((NX, NY, 2 * ZL), f32)
        two = jax.ShapeDtypeStruct((2,), f32)

        def body(*refs):
            kernel(gx_count, gy_count, *refs)

        inside = pl.BlockSpec(memory_space=pltpu.VMEM)
        made = pl.pallas_call(
            body,
            out_shape=(pltpu.VMEM((NX, 2, NY, ZL), f32), pltpu.VMEM((NX, 2, NY, ZL), f32), two, two),
            in_specs=[any_] * 9,
            out_specs=(inside, inside, smem, smem),
            scratch_shapes=scratch,
            compiler_params=pltpu.CompilerParams(
                collective_id=0, has_side_effects=True, vmem_limit_bytes=61 * 1024 * 1024
            ),
        )(*args[:3], *args[7:], *args[3:7])
        return tuple(v.transpose(0, 2, 1, 3).reshape(NX, NY, 2 * ZL) for v in made[:2]) + tuple(made[2:])

    return jax.shard_map(
        local,
        mesh=mesh,
        in_specs=(
            P("gx", "gy", None),
            P("gx", "gy", None),
            P(None, "gx", "gy", None),
            P(("gx", "gy")),
            P(("gx", "gy")),
            P("gx", "gy", None),
            P("gx", "gy", None),
            P("gx", "gy", None),
            P("gx", "gy", None),
        ),
        out_specs=(P("gx", "gy", None), P("gx", "gy", None), P(("gx", "gy")), P(("gx", "gy"))),
        check_vma=False,
    )
```

```python
import jax
import jax.numpy as jnp
from jax import lax
from jax.experimental import pallas as pl
from jax.experimental.pallas import tpu as pltpu
from jax.sharding import PartitionSpec as P

MESH = pl.DeviceIdType.MESH
STEPS = 4
DT = 0.05
EPS_W = 0.1
NX, NY, ZL = 32, 32, 128
Y0 = 8
YP = 48
YT = NY // 8
TILE = 32

XX, XY, XZ, YZ, YY, ZZ = range(6)

SIN = (0.9999999954376937, -0.16666657521871267, 0.008333039791882324, -0.0001980823258586027, 2.603293610558432e-06)
COS = (
    0.9999999997626233,
    -0.4999999931520218,
    0.041666634639589036,
    -0.0013888340619260778,
    2.4759088421126325e-05,
    -2.6032335044441285e-07,
)


def poly(z, coefs):
    total = coefs[-1] * z + coefs[-2]
    for value in coefs[-3::-1]:
        total = total * z + value
    return total


def sincos(x):
    t = (1.5707963705062866 - jnp.abs(x)) - 4.371139000186241e-08
    z = t * t
    cosine = t * poly(z, SIN)
    size = poly(z, COS)
    return jnp.where(x < 0.0, -size, size), cosine


def products(theta, phi):
    st, ct = sincos(theta)
    sp, cp = sincos(phi)
    fx, fy, fz = cp * ct, cp * st, sp
    return {XX: fx * fx, YY: fy * fy, ZZ: fz * fz, XY: fx * fy, XZ: fx * fz, YZ: fy * fz}


def lane():
    return lax.broadcasted_iota(jnp.int32, (8, ZL), 1)


def z_up(h0, h1):
    last = lane() == ZL - 1
    r0, r1 = pltpu.roll(h0, ZL - 1, 1), pltpu.roll(h1, ZL - 1, 1)
    return jnp.where(last, r1, r0), jnp.where(last, 0.0, r1)


def z_down(h0, h1, edge=0.0):
    first = lane() == 0
    r0, r1 = pltpu.roll(h0, 1, 1), pltpu.roll(h1, 1, 1)
    return jnp.where(first, edge, r0), jnp.where(first, r0, r1)


def pair(fn):
    return fn(0), fn(1)


def kernel(
    gx_count,
    gy_count,
    pot,
    rec,
    fib,
    cot_p,
    cot_r,
    sig_l_in,
    sig_t_in,
    region_in,
    tissue_in,
    ulast,
    llast,
    out_l,
    out_t,
    u0,
    u1,
    u2,
    u3,
    l4,
    l3,
    l2,
    l1,
    r0,
    r1_,
    r2_,
    r3,
    ww,
    mu,
    fp,
    dx,
    dy,
    dz,
    dzm,
    ex,
    fhx,
    fhy,
    tt,
    bb,
    py,
    ay,
    px,
    gzs,
    dzs,
    ysend,
    halo,
    crecv,
    fysend,
    frecv,
    cfd,
    cfh,
    cfo,
    kf,
    tinfo,
    trecv,
    g1send,
    g1recv,
    quad,
    rsend,
    rrecv,
    rg,
    sv,
    acc,
    sig_l,
    sig_t,
    region,
    tissue,
    load_sem,
    small_sem,
    xs,
    xr,
    fs,
    fr,
    ts,
    tr,
    g1s,
    g1r,
    g2s,
    g2r,
    r1s,
    r1r,
    r2s,
    r2r,
):
    gx, gy = lax.axis_index("gx"), lax.axis_index("gy")
    has = {"l": gx > 0, "r": gx < gx_count - 1, "d": gy > 0, "u": gy < gy_count - 1}
    us = (u0, u1, u2, u3)
    ls = (l4, l3, l2, l1)
    rs = (r0, r1_, r2_, r3)
    fields = us + ls
    data = pl.ds(Y0, NY)
    names = "lrdu"
    corner_list = (("l", "d"), ("l", "u"), ("r", "d"), ("r", "u"))
    step_of = {"l": (-1, 0), "r": (1, 0), "d": (0, -1), "u": (0, 1)}

    def loads(index, src, dst, padded):
        out = []
        for h in range(2):
            s = src.at[:, :, pl.ds(h * ZL, ZL)]
            d = dst.at[pl.ds(1, NX), h, data, :] if padded else dst.at[:, h]
            out.append(pltpu.make_async_copy(s, d, load_sem.at[index, h]))
        return out

    copies = [
        loads(0, fib.at[0], tt, False),
        loads(1, fib.at[1], bb, True),
        loads(2, pot, u0, True),
        loads(3, cot_p, l4, True),
        loads(4, rec, ww, False),
        loads(5, cot_r, mu, False),
    ]
    small = [
        pltpu.make_async_copy(a, b, small_sem.at[i])
        for i, (a, b) in enumerate(((sig_l_in, sig_l), (sig_t_in, sig_t), (region_in, region), (tissue_in, tissue)))
    ]
    for copy in small:
        copy.start()
    for group in copies:
        for copy in group:
            copy.start()

    barrier = pltpu.get_barrier_semaphore()

    def both(a, b):
        return jnp.logical_and(has[a], has[b])

    def target(*sides):
        return (gx + sum(step_of[s][0] for s in sides), gy + sum(step_of[s][1] for s in sides))

    for a, b in corner_list:

        @pl.when(both(a, b))
        def _(a=a, b=b):
            pl.semaphore_signal(barrier, inc=1, device_id=target(a, b), device_id_type=MESH)

    @pl.loop(1, gy_count)
    def _(k):
        pl.semaphore_signal(barrier, inc=1, device_id=(gx, lax.rem(gy + k, gy_count)), device_id_type=MESH)

    @pl.loop(1, gx_count)
    def _(k):
        pl.semaphore_signal(barrier, inc=1, device_id=(lax.rem(gx + k, gx_count), gy), device_id_type=MESH)

    gxi = (gx > 0).astype(jnp.int32) + (gx < gx_count - 1).astype(jnp.int32)
    gyi = (gy > 0).astype(jnp.int32) + (gy < gy_count - 1).astype(jnp.int32)

    def remote(src, dst, send, recv, device):
        return pltpu.make_async_remote_copy(
            src_ref=src, dst_ref=dst, send_sem=send, recv_sem=recv, device_id=device, device_id_type=MESH
        )

    zero = jnp.zeros((8, ZL), jnp.float32)
    face0 = jnp.zeros((2, NY, ZL), jnp.float32)
    line0 = jnp.zeros((1, ZL), jnp.float32)
    for f in fields:
        f[0, :, Y0 : Y0 + NY, :] = face0
        f[NX + 1, :, Y0 : Y0 + NY, :] = face0
    bb[0, :, Y0 : Y0 + NY, :] = face0

    @pl.loop(1, NX + 1)
    def _(p):
        for h in range(2):
            for f in fields:
                f[p, h, Y0 - 1 : Y0, :] = line0
                f[p, h, Y0 + NY : Y0 + NY + 1, :] = line0
            ay[p, h, Y0 - 1 : Y0, :] = line0
            py[p, h, Y0 + NY : Y0 + NY + 1, :] = line0

    for i, name in enumerate(names):

        @pl.when(jnp.logical_not(has[name]))
        def _(i=i):
            for k in range(8):
                halo[k, i, :, Y0 : Y0 + NY, :] = face0
            for c in range(3):
                frecv[i, c] = face0
            trecv[i] = zero

    for c, (a, b) in enumerate(corner_list):

        @pl.when(jnp.logical_not(both(a, b)))
        def _(c=c):
            for k in range(8):
                crecv[k, c] = jnp.zeros((2, 8, ZL), jnp.float32)

    for i in range(4):
        for h in range(2):
            cfo[i, 0, h, Y0 - 1 : Y0, :] = line0
            cfo[i, 0, h, Y0 + NY : Y0 + NY + 1, :] = line0
    acc[...] = jnp.zeros_like(acc)

    for copy in small:
        copy.wait()
    lanes = lane()
    tile_of = lanes // TILE

    def lane_vector(ref, h):
        value = zero
        for k in range(4):
            value = jnp.where(tile_of == k, ref[0, 0, 4 * h + k].astype(jnp.float32), value)
        return value

    own_r = [lane_vector(region, h) for h in range(2)]
    own_t = [lane_vector(tissue, h) for h in range(2)]
    sub = lax.broadcasted_iota(jnp.int32, (8, ZL), 0)
    subf = sub.astype(jnp.float32)
    tinfo[...] = jnp.where(
        sub == 0, own_r[0], jnp.where(sub == 1, own_r[1], jnp.where(sub == 2, own_t[0], own_t[1]))
    )
    value = jnp.where(
        lanes < 64, jnp.where(sub == 2 * gy, sig_l[0], sig_l[1]), jnp.where(sub == 2 * gy, sig_t[0], sig_t[1])
    )
    mine = jnp.where(jnp.logical_or(sub == 2 * gy, sub == 2 * gy + 1), value, 0.0)
    g1send[...] = mine

    other = (1, 0, 3, 2)

    def start(list_):
        for cond, _, copy in list_:

            @pl.when(cond)
            def _(copy=copy):
                copy.start()

    def wait_recv(list_):
        for _, cond, copy in list_:

            @pl.when(cond)
            def _(copy=copy):
                copy.wait_recv()

    def wait_send(list_):
        for cond, _, copy in list_:

            @pl.when(cond)
            def _(copy=copy):
                copy.wait_send()

    def to_faces(sources, dest, send, recv):
        return [
            (has[s], has[names[other[i]]], remote(sources[i], dest(other[i]), send(i), recv(other[i]), target(s)))
            for i, s in enumerate(names)
        ]

    def tile_copies():
        return to_faces([tinfo] * 4, lambda i: trecv.at[i], lambda i: ts.at[i], lambda i: tr.at[i])

    def fiber_exchange():
        first = pl.ds(0, 3)
        sources = [fp.at[first, 1, :, data, :], fp.at[first, NX, :, data, :], fysend.at[0], fysend.at[1]]
        return to_faces(sources, lambda i: frecv.at[i], lambda i: fs.at[i], lambda i: fr.at[i])

    def exchange(k):
        f = fields[k]
        sources = [f.at[1, :, data, :], f.at[NX, :, data, :], ysend.at[k, 0, :, data, :], ysend.at[k, 1, :, data, :]]
        out = to_faces(
            sources, lambda i: halo.at[k, i, :, data, :], lambda i: xs.at[k, i], lambda i: xr.at[k, i]
        )
        for c, (a, b) in enumerate(corner_list):
            xrow = Y0 if a == "l" else Y0 + NX - 8
            src = ysend.at[k, 0 if b == "d" else 1, :, pl.ds(xrow, 8), :]
            copy = remote(src, crecv.at[k, 3 - c], xs.at[k, 4 + c], xr.at[k, 7 - c], target(a, b))
            out.append((both(a, b), both(*corner_list[3 - c]), copy))
        return out

    def g1(k):
        return remote(g1send, g1recv.at[k], g1s.at[k], g1r.at[k], (gx, lax.rem(gy + k, gy_count)))

    def g2(k):
        return remote(quad.at[0], quad.at[k], g2s, g2r, (lax.rem(gx + k, gx_count), gy))

    def wait_load(index):
        for copy in copies[index]:
            copy.wait()

    def pack_rows(f, k):
        @pl.loop(0, NX)
        def _(x):
            for h in range(2):
                ysend[k, 0, h, pl.ds(x + Y0, 1), :] = f[x + 1, h, Y0 : Y0 + 1, :]
                ysend[k, 1, h, pl.ds(x + Y0, 1), :] = f[x + 1, h, Y0 + NY - 1 : Y0 + NY, :]

    def trig(x):
        for yt in range(YT):
            y = yt * 8
            for h in range(2):
                got = products(tt[x, h, y : y + 8, :], bb[x + 1, h, Y0 + y : Y0 + y + 8, :])
                for c in range(6):
                    fp[c, x + 1, h, Y0 + y : Y0 + y + 8, :] = got[c]
                for i, c in enumerate((YY, XY, YZ)):
                    if yt == 0:
                        fysend[0, i, h, pl.ds(x, 1), :] = got[c][0:1]
                    if yt == YT - 1:
                        fysend[1, i, h, pl.ds(x, 1), :] = got[c][7:8]

    wait_load(0)
    wait_load(1)
    pl.loop(0, 2)(lambda i: trig(i * (NX - 1)))
    pl.loop(1, 8)(trig)
    pl.semaphore_wait(barrier, gx_count - 1 + gy_count - 1 + gxi * gyi)
    for k in range(1, gy_count):
        g1(k).start()
    start(tile_copies())
    start(fiber_exchange()[:2])
    pl.loop(8, 20)(trig)
    quad_own = mine
    for k in range(1, gy_count):
        g1(k).wait_recv()
        quad_own = quad_own + g1recv[k]
    quad[0] = quad_own

    @pl.loop(1, gx_count)
    def _(k):
        g2(k).start()

    pl.loop(20, NX - 1)(trig)
    start(fiber_exchange()[2:])
    wait_load(2)
    pack_rows(u0, 0)
    start(exchange(0))
    wait_load(3)
    pack_rows(l4, 4)

    wait_recv(tile_copies())
    remote(quad.at[pl.ds(1, gx_count - 1)], quad.at[pl.ds(1, gx_count - 1)], g2s, g2r, (gx, gy)).wait_recv()
    regions = list(own_r)
    flags = list(own_t)
    for i in range(4):
        for h in range(2):
            regions.append(jnp.broadcast_to(trecv[i, h : h + 1, :], (8, ZL)))
            flags.append(jnp.broadcast_to(trecv[i, 2 + h : 3 + h, :], (8, ZL)))

    def lookup(k, sums):
        tile = quad[k]
        turned = pltpu.roll(tile, 64, 1)
        low = lanes < 64
        long_, trans = jnp.where(low, tile, turned), jnp.where(low, turned, tile)
        group = lax.rem(gx - k + gx_count, gx_count)
        ids = subf + (8 * group).astype(jnp.float32)
        new = []
        for i in range(10):
            hit = regions[i] == ids
            new.append(jnp.where(hit, long_, sums[2 * i]))
            new.append(jnp.where(hit, trans, sums[2 * i + 1]))
        return tuple(new)

    sums = lax.fori_loop(0, gx_count, lookup, (zero,) * 20)
    for i in range(10):
        s_l = jnp.broadcast_to(jnp.sum(sums[2 * i], axis=0, keepdims=True), (8, ZL)) * flags[i]
        s_t = jnp.broadcast_to(jnp.sum(sums[2 * i + 1], axis=0, keepdims=True), (8, ZL)) * flags[i]
        sv[i // 2, 0, i % 2] = s_t
        sv[i // 2, 1, i % 2] = s_l - s_t

    c_pair = 0.25 * DT
    c_axis = 0.5 * DT
    st = pair(lambda h: sv[0, 0, h])
    ee = pair(lambda h: sv[0, 1, h])
    ea = pair(lambda h: c_axis * ee[h])
    ep = pair(lambda h: c_pair * ee[h])
    s2 = pair(lambda h: DT * st[h])

    def coefficients(p):
        for yt in range(YT):
            y = yt * 8
            r = slice(Y0 + y, Y0 + y + 8)
            q = slice(y, y + 8)
            dzz = []
            for h in range(2):
                sum_x = fp[XX, p, h, r, :] + fp[XX, p + 1, h, r, :]
                sum_y = fp[YY, p, h, r, :] + fp[YY, p, h, Y0 + y + 1 : Y0 + y + 9, :]
                if yt == YT - 1:
                    sum_y = jnp.where(sub == 7, 0.0, sum_y)
                fhx[p, h, q, :] = sum_x
                fhy[p, h, q, :] = sum_y
                dx[p, h, q, :] = s2[h] + ea[h] * sum_x
                dy[p, h, q, :] = s2[h] + ea[h] * sum_y
                dzz.append(c_axis * st[h] + ea[h] * fp[ZZ, p, h, r, :])
                for i, c in enumerate((XY, XZ, YZ)):
                    ex[i, p, h, q, :] = ep[h] * fp[c, p, h, r, :]
            up = z_up(*dzz)
            for h in range(2):
                dz[p, h, q, :] = dzz[h] + up[h]
            dzm[p, q, :] = dzz[0]
            above = z_up(*pair(lambda h: fp[ZZ, p, h, r, :]))
            for h in range(2):
                fp[YY, p, h, r, :] = above[h]

    pl.loop(1, NX + 1)(coefficients)
    wait_recv(fiber_exchange())

    def own_products(i, c, h, t):
        if i < 2:
            return fp[(XX, XY, XZ)[c], 1 if i == 0 else NX, h, Y0 + t * 8 : Y0 + t * 8 + 8, :]
        return fysend[i - 2, c, h, t * 8 : t * 8 + 8, :]

    for i in range(4):
        for h in range(2):
            st_n, e_n = sv[1 + i, 0, h], sv[1 + i, 1, h]
            for t in range(4):
                q = slice(t * 8, t * 8 + 8)
                total = (st_n + e_n * frecv[i, 0, h, q, :]) + (st[h] + ee[h] * own_products(i, 0, h, t))
                cfd[i, h, q, :] = c_axis * total
                if i == 1:
                    dx[NX, h, q, :] = c_axis * total
                    fhx[NX, h, q, :] = zero
                for j in range(2):
                    cfh[i, j, h, q, :] = c_pair * e_n * frecv[i, 1 + j, h, q, :]
                    cfo[i, j, h, Y0 + t * 8 : Y0 + t * 8 + 8, :] = ep[h] * own_products(i, 1 + j, h, t)

    for i in range(4):
        sign = -1.0 if i in (0, 2) else 1.0
        for t in range(4):
            q = slice(t * 8, t * 8 + 8)
            r = Y0 + t * 8
            turn = pair(lambda h: cfo[i, 1, h, r : r + 8, :])
            above, below = z_up(*turn), z_down(*turn)
            for h in range(2):
                kf[i, 0, h, q, :] = sign * (cfh[i, 0, h, q, :] + cfo[i, 0, h, r + 1 : r + 9, :])
                kf[i, 1, h, q, :] = sign * (cfh[i, 0, h, q, :] + cfo[i, 0, h, r - 1 : r + 7, :])
                kf[i, 2, h, q, :] = sign * (cfh[i, 1, h, q, :] + above[h])
                kf[i, 3, h, q, :] = sign * (cfh[i, 1, h, q, :] + below[h])

    for x in range(NX):
        for h in range(2):
            dy[x + 1, h, NY - 1 : NY, :] = cfd[3, h, x : x + 1, :]

    def rows(y, shift=0):
        return slice(Y0 + y + shift, Y0 + y + shift + 8)

    def near(f, p, y, along_z=True):
        c = pair(lambda h: f[p, h, rows(y), :])
        xp = pair(lambda h: f[p + 1, h, rows(y), :])
        xm = pair(lambda h: f[p - 1, h, rows(y), :])
        yp = pair(lambda h: f[p, h, rows(y, 1), :])
        ym = pair(lambda h: f[p, h, rows(y, -1), :])
        around = (c, xp, xm, yp, ym)
        return (*around, z_up(*c), z_down(*c)) if along_z else around

    def add_sums(sums, n, p, y, h, c, v, around, flux, diff):
        q = slice(y, y + 8)
        v_x, v_y, w_x, w_y = around
        cross = v_x * flux[0] + v_y * flux[1] + gzs[n, p - 1, h, q, :] * flux[2]
        m_x, m_y, m_z = diff[0] * w_x, diff[1] * w_y, diff[2] * dzs[n, p - 1, h, q, :]
        sums[h] = sums[h] + (
            (fhx[p, h, q, :] * m_x + fhy[p, h, q, :] * m_y) + (fp[ZZ, p, h, rows(y), :] * m_z + 0.5 * cross)
        )
        sums[2 + h] = sums[2 + h] + (m_x + m_y)
        sums[4 + h] = sums[4 + h] + m_z
        sums[6 + h] = sums[6 + h] + fp[YY, p, h, rows(y), :] * m_z
        if h == 0:
            m_0 = c[0] * v[0]
            sums[8] = sums[8] + fp[ZZ, p, 0, rows(y), :] * m_0
            sums[9] = sums[9] + m_0

    def keep_sums(sums):
        over_l = z_down(sums[6], sums[7], edge=sums[8])
        over_t = z_down(sums[4], sums[5], edge=sums[9])
        for h in range(2):
            acc[h] = acc[h] + (sums[h] + over_l[h])
            acc[2 + h] = acc[2 + h] + (2.0 * sums[2 + h] + (sums[4 + h] + over_t[h]))

    def only_sums(k, n):
        f, u = fields[k], us[n]

        def body(p, carry):
            sums = list(carry)
            for yt in range(YT):
                y = yt * 8
                c, xp, xm, yp, ym, zp, zm = near(f, p, y)
                v, vxp, vxm, vyp, vym = near(u, p, y, False)
                for h in range(2):
                    e_xy, e_xz, e_yz = (fp[i, p, h, rows(y), :] for i in (XY, XZ, YZ))
                    g_x, g_y, g_z = xp[h] - xm[h], yp[h] - ym[h], zp[h] - zm[h]
                    flux = (e_xy * g_y + e_xz * g_z, e_xy * g_x + e_yz * g_z, e_xz * g_x + e_yz * g_y)
                    diff = (xp[h] - c[h], yp[h] - c[h], zp[h] - c[h])
                    around = (vxp[h] - vxm[h], vyp[h] - vym[h], vxp[h] - v[h], vyp[h] - v[h])
                    add_sums(sums, n, p, y, h, c, v, around, flux, diff)
            return tuple(sums)

        keep_sums(lax.fori_loop(1, NX + 1, body, (zero,) * 10))

    def stage_a(f, p, yt, react, backs, n, sens=None):
        y = yt * 8
        q = slice(y, y + 8)
        c, xp, xm, yp, ym, zp, zm = near(f, p, y)
        own = react(p, y, c)
        if sens is not None:
            u, sums = sens
            v, vxp, vxm, vyp, vym = near(u, p, y, False)
        local, pz, az = [], [], []
        for h in range(2):
            g_x, g_y, g_z = xp[h] - xm[h], yp[h] - ym[h], zp[h] - zm[h]
            if sens is None:
                e_xy, e_xz, e_yz = (ex[i, p, h, q, :] for i in range(3))
            else:
                e_xy, e_xz, e_yz = (fp[i, p, h, rows(y), :] for i in (XY, XZ, YZ))
            p_x = e_xy * g_y + e_xz * g_z
            p_y = e_xy * g_x + e_yz * g_z
            p_z = e_xz * g_x + e_yz * g_y
            d_x, d_y, d_z = xp[h] - c[h], yp[h] - c[h], zp[h] - c[h]
            if sens is None and n is not None:
                gzs[n, p - 1, h, q, :] = g_z
                dzs[n, p - 1, h, q, :] = d_z
            if sens is not None:
                around = (vxp[h] - vxm[h], vyp[h] - vym[h], vxp[h] - v[h], vyp[h] - v[h])
                add_sums(sums, n, p, y, h, c, v, around, (p_x, p_y, p_z), (d_x, d_y, d_z))
                p_x, p_y, p_z = ep[h] * p_x, ep[h] * p_y, ep[h] * p_z
            f_x = dx[p, h, q, :] * d_x
            f_y = dy[p, h, q, :] * d_y
            f_z = dz[p, h, q, :] * d_z
            back = backs[yt][h]
            bb[p, h, rows(y), :] = f_x + p_x
            py[p, h, rows(y), :] = p_y
            ay[p, h, rows(y), :] = f_y + p_y
            pz.append(p_z)
            az.append(f_z + p_z)
            px[p, h, q, :] = p_x
            local.append((own[h] + f_x) + (f_y - back))
            local[h] = local[h] + f_z
        up = z_up(*pz)
        down = z_down(*az, edge=dzm[p, q, :] * c[0])
        for h in range(2):
            tt[p - 1, h, q, :] = local[h] + (up[h] - down[h])

    def stage_b(p, yt, put, last=False):
        y = yt * 8
        for h in range(2):
            value = tt[p - 1, h, y : y + 8, :] + (py[p, h, rows(y, 1), :] - ay[p, h, rows(y, -1), :])
            put(p, h, yt, value if last else value + px[p + 1, h, y : y + 8, :])

    def apply(k, n, react, put, u=None):
        f = fields[k]

        def plane(p, running):
            backs = [pair(lambda h: bb[p - 1, h, rows(yt * 8), :]) for yt in range(YT)]
            for yt in range(YT):
                stage_a(f, p, yt, react, backs, n, None if u is None else (u, running))

        def body(p, carry, complete=True):
            running = list(carry)
            if complete:
                for yt in range(YT):
                    stage_b(p - 2, yt, put)
            plane(p, running)
            return tuple(running)

        sums = (zero,) * (0 if u is None else 10)
        sums = lax.fori_loop(1, 3, lambda p, carry: body(p, carry, False), sums)
        sums = lax.fori_loop(3, NX + 1, body, sums)
        if u is not None:
            keep_sums(sums)
        for yt in range(YT):
            stage_b(NX - 1, yt, put)
        for yt in range(YT):
            stage_b(NX, yt, put, True)

    def put_to(ref, slot, plane0, row0):
        def put(p, h, yt, value):
            ref[p - 1 + plane0, h, row0 + yt * 8 : row0 + yt * 8 + 8, :] = value
            if yt == 0:
                ysend[slot, 0, h, pl.ds(p - 1 + Y0, 1), :] = value[0:1]
            if yt == YT - 1:
                ysend[slot, 1, h, pl.ds(p - 1 + Y0, 1), :] = value[7:8]

        return put

    def install(k):
        for c, (a, b) in enumerate(corner_list):
            at = 7 if a == "l" else 0
            for h in range(2):
                v = crecv[k, c, h, at : at + 1, :]
                row = Y0 - 1 if b == "d" else Y0 + NY
                halo[k, names.index(a), h, row : row + 1, :] = v
                row = Y0 - 1 if a == "l" else Y0 + NX
                halo[k, names.index(b), h, row : row + 1, :] = v
        for s in range(2):
            row = Y0 if s == 0 else Y0 + NY - 1
            for h in range(2):
                ysend[k, s, h, Y0 - 1 : Y0, :] = halo[k, 0, h, row : row + 1, :]
                ysend[k, s, h, Y0 + NX : Y0 + NX + 1, :] = halo[k, 1, h, row : row + 1, :]

    def layer(k, i, h, r):
        if i < 2:
            return fields[k][1 if i == 0 else NX, h, r, :]
        return ysend[k, i - 2, h, r, :]

    def delta(k, i, t):
        lo = i in (0, 2)
        y = t * 8
        q = slice(y, y + 8)
        c = pair(lambda h: halo[k, i, h, rows(y), :])
        zp, zm = z_up(*c), z_down(*c)
        out = []
        for h in range(2):
            bp, bm = halo[k, i, h, rows(y, 1), :], halo[k, i, h, rows(y, -1), :]
            total = kf[i, 0, h, q, :] * bp - kf[i, 1, h, q, :] * bm
            total = total + (kf[i, 2, h, q, :] * zp[h] - kf[i, 3, h, q, :] * zm[h])
            edge = c[h] - layer(k, i, h, rows(y)) if lo else c[h]
            out.append(cfd[i, h, q, :] * edge + total)
        return out

    def finish(k, ref, slot, plane0, row0, arrived=False):
        if not arrived:
            wait_recv(exchange(k))
            install(k)
        for i, plane in ((0, plane0), (1, plane0 + NX - 1)):
            for t in range(4):
                d = delta(k, i, t)
                for h in range(2):
                    r = slice(row0 + t * 8, row0 + t * 8 + 8)
                    ref[plane, h, r, :] = ref[plane, h, r, :] + d[h]
            x = Y0 if i == 0 else Y0 + NX - 1
            for h in range(2):
                ysend[slot, 0, h, x : x + 1, :] = ref[plane, h, row0 : row0 + 1, :]
                ysend[slot, 1, h, x : x + 1, :] = ref[plane, h, row0 + NY - 1 : row0 + NY, :]
        for i in (2, 3):
            for t in range(4):
                d = delta(k, i, t)
                for h in range(2):
                    ysend[slot, i - 2, h, rows(t * 8), :] = ysend[slot, i - 2, h, rows(t * 8), :] + d[h]
        for x in (0, NX - 1):
            write_back(x, ref, slot, plane0, row0)

    def write_back(x, ref, slot, plane0, row0):
        for h in range(2):
            ref[x + plane0, h, row0 : row0 + 1, :] = ysend[slot, 0, h, x + Y0 : x + Y0 + 1, :]
            ref[x + plane0, h, row0 + NY - 1 : row0 + NY, :] = ysend[slot, 1, h, x + Y0 : x + Y0 + 1, :]

    def write_back_rest(ref, slot, plane0, row0):
        for x in range(1, NX - 1):
            write_back(x, ref, slot, plane0, row0)

    wait_load(4)
    wait_load(5)
    for n in range(STEPS):

        def react(p, y, c, n=n):
            q = slice(y, y + 8)
            out = []
            for h in range(2):
                w = ww[p - 1, h, q, :]
                u = c[h]
                part = (8.0 * DT) * u
                turn = 8.0 * DT * 1.15 - part
                poly_ = u * turn
                rate = ((1.0 - 8.0 * DT * 0.15) - DT * w) + poly_
                out.append(u * rate)
                rs[n][p - 1, h, q, :] = rate + u * (turn - part)
                if n < STEPS - 1:
                    ww[p - 1, h, q, :] = (1.0 - DT * EPS_W) * w + EPS_W * poly_
            return out

        if n < STEPS - 1:
            place = (fields[n + 1], n + 1, 1, Y0)
        else:
            place = (ulast, 8, 0, 0)
        apply(n, n, react, put_to(*place))
        finish(n, *place)
        if n < STEPS - 1:
            start(exchange(n + 1))
        if n == 0:
            start(exchange(4))
        write_back_rest(*place)

    c_mu = 16.0 * DT * EPS_W

    def face_sums(n, k):
        sums = [zero] * 4
        for i in range(4):
            lo = i in (0, 2)
            for t in range(4):
                y = t * 8
                for_z = [pair(lambda h: layer(f, i, h, rows(y))) for f in (n, k)]
                zs = [(z_up(*c), z_down(*c)) for c in for_z]
                for h in range(2):
                    f_aa, f_ab, f_az = (own_products(i, c, h, t) for c in range(3))
                    flux = [
                        f_ab * (layer(f, i, h, rows(y, 1)) - layer(f, i, h, rows(y, -1))) + f_az * (z[0][h] - z[1][h])
                        for f, z in zip((n, k), zs)
                    ]
                    h_u, h_l = halo[n, i, h, rows(y), :], halo[k, i, h, rows(y), :]
                    o_u, o_l = for_z[0][h], for_z[1][h]
                    m = (o_u - h_u) * (o_l - h_l)
                    cross = 0.5 * (h_u * flux[1] + h_l * flux[0])
                    sums[h] = sums[h] + (f_aa * m - cross if lo else f_aa * m + cross)
                    sums[2 + h] = sums[2 + h] + (m if lo else m - 2.0 * (o_u * o_l))
        for i in range(4):
            acc[i] = acc[i] + sums[i]

    def r1(k):
        return remote(rsend.at[k], rrecv.at[k], r1s, r1r, (lax.rem(gx + k, gx_count), gy))

    def r2(k):
        return remote(rg.at[0], rg.at[k], r2s.at[k], r2r.at[k], (gx, lax.rem(gy + k, gy_count)))

    def second_stage():
        rest = pl.ds(1, gx_count - 1)
        remote(rsend.at[rest], rrecv.at[rest], r1s, r1r, (gx, gy)).wait_recv()
        total = lax.fori_loop(0, gx_count, lambda k, t: t + rrecv[k], zero)
        rg[0] = total
        for k in range(1, gy_count):
            r2(k).start()
        return total

    def send_sums():
        scale = -0.5 * DT / TILE**1.5
        flat = []
        for h in range(2):
            s_l = jnp.broadcast_to(jnp.sum(acc[h], axis=0, keepdims=True), (8, ZL))
            s_a = jnp.broadcast_to(jnp.sum(acc[2 + h], axis=0, keepdims=True), (8, ZL))
            flat.append((scale * own_t[h] * s_l, scale * own_t[h] * (s_a - s_l)))

        def parts_of(group):
            ids = subf + (8 * group).astype(jnp.float32)
            tot = []
            for j in range(2):
                v = sum(jnp.where(own_r[h] == ids, flat[h][j], 0.0) for h in range(2))
                tot.append(v + pltpu.roll(v, 64, 1))
            return jnp.where(lanes < 64, tot[0], tot[1])

        rrecv[0] = parts_of(gx)

        @pl.loop(1, gx_count)
        def _(k):
            rsend[k] = parts_of(lax.rem(gx + k, gx_count))
            r1(k).start()

    for n in range(STEPS - 1, -1, -1):
        k = 4 + STEPS - 1 - n

        def react(p, y, c, n=n):
            q = slice(y, y + 8)
            out = []
            for h in range(2):
                u = us[n][p, h, rows(y), :]
                m = mu[p - 1, h, q, :]
                if n == STEPS - 1:
                    m = c_mu * m
                out.append(c[h] * rs[n][p - 1, h, q, :] - (u - 0.575) * m)
                if n > 0:
                    mu[p - 1, h, q, :] = (1.0 - DT * EPS_W) * m - ((DT * c_mu) * c[h]) * u
            return out

        place = (fields[k + 1], k + 1, 1, Y0) if n > 0 else (llast, 9, 0, 0)
        if n > 0:
            apply(k, n, react, put_to(*place), us[n])
            finish(k, *place)
            start(exchange(k + 1))
            write_back_rest(*place)
            face_sums(n, k)
        else:
            only_sums(7, 0)
            wait_recv(exchange(7))
            install(7)
            face_sums(0, 7)
            send_sums()
            apply(k, None, react, put_to(*place))
            total = second_stage()
            finish(k, *place, True)
            write_back_rest(*place)

    wait_send(tile_copies())
    wait_send(fiber_exchange())
    for k in range(8):
        wait_send(exchange(k))
    for k in range(1, gy_count):
        g1(k).wait_send()
    remote(quad.at[pl.ds(1, gx_count - 1)], quad.at[pl.ds(1, gx_count - 1)], g2s, g2r, (gx, gy)).wait_send()

    for k in range(1, gy_count):
        r2(k).wait_recv()
        total = total + rg[k]
    for j in range(2):
        mine_row = sub == 2 * gy + j
        out_l[j] = jnp.sum(jnp.where(jnp.logical_and(mine_row, lanes < 64), total, 0.0))
        out_t[j] = jnp.sum(jnp.where(jnp.logical_and(mine_row, lanes >= 64), total, 0.0))
    for k in range(1, gy_count):
        r2(k).wait_send()
    remote(rsend.at[pl.ds(1, gx_count - 1)], rrecv.at[pl.ds(1, gx_count - 1)], r1s, r1r, (gx, gy)).wait_send()


def solution(mesh):
    gx_count, gy_count = mesh.shape["gx"], mesh.shape["gy"]

    def local(*args):
        any_, smem = pl.BlockSpec(memory_space=pl.ANY), pl.BlockSpec(memory_space=pltpu.SMEM)
        f32 = jnp.float32
        padded = pltpu.VMEM((NX + 2, 2, YP, ZL), f32)
        plain = pltpu.VMEM((NX, 2, NY, ZL), f32)
        dma = pltpu.SemaphoreType.DMA
        def vmem(*shape):
            return pltpu.VMEM(shape, f32)

        scratch = [padded] * 8 + [plain] * 4 + [plain] * 2
        scratch += [
            vmem(6, NX + 2, 2, YP, ZL),
            vmem(NX + 1, 2, NY, ZL),
            vmem(NX + 1, 2, NY, ZL),
            vmem(NX + 1, 2, NY, ZL),
            vmem(NX + 1, NY, ZL),
            vmem(3, NX + 1, 2, NY, ZL),
            vmem(NX + 1, 2, NY, ZL),
            vmem(NX + 1, 2, NY, ZL),
            plain,
            padded,
            padded,
            padded,
            vmem(NX + 1, 2, NY, ZL),
            vmem(STEPS, NX, 2, NY, ZL),
            vmem(STEPS, NX, 2, NY, ZL),
            vmem(10, 2, 2, YP, ZL),
            vmem(8, 4, 2, YP, ZL),
            vmem(8, 4, 2, 8, ZL),
            vmem(2, 3, 2, NX, ZL),
            vmem(4, 3, 2, NX, ZL),
            vmem(4, 2, NX, ZL),
            vmem(4, 2, 2, NX, ZL),
            vmem(4, 2, 2, YP, ZL),
            vmem(4, 4, 2, NX, ZL),
            vmem(8, ZL),
            vmem(4, 8, ZL),
            vmem(8, ZL),
            vmem(gy_count, 8, ZL),
            vmem(gx_count, 8, ZL),
            vmem(gx_count, 8, ZL),
            vmem(gx_count, 8, ZL),
            vmem(gy_count, 8, ZL),
            vmem(5, 2, 2, 8, ZL),
            vmem(4, 8, ZL),
            pltpu.SMEM((2,), f32),
            pltpu.SMEM((2,), f32),
            pltpu.SMEM((1, 1, 8), jnp.int32),
            pltpu.SMEM((1, 1, 8), jnp.int32),
            dma((6, 2)),
            dma((4,)),
            dma((8, 8)),
            dma((8, 8)),
            dma((4,)),
            dma((4,)),
            dma((4,)),
            dma((4,)),
            dma((gy_count,)),
            dma((gy_count,)),
            dma(()),
            dma(()),
            dma(()),
            dma(()),
            dma((gy_count,)),
            dma((gy_count,)),
        ]
        field = jax.ShapeDtypeStruct((NX, NY, 2 * ZL), f32)
        two = jax.ShapeDtypeStruct((2,), f32)

        def body(*refs):
            kernel(gx_count, gy_count, *refs)

        inside = pl.BlockSpec(memory_space=pltpu.VMEM)
        made = pl.pallas_call(
            body,
            out_shape=(pltpu.VMEM((NX, 2, NY, ZL), f32), pltpu.VMEM((NX, 2, NY, ZL), f32), two, two),
            in_specs=[any_] * 9,
            out_specs=(inside, inside, smem, smem),
            scratch_shapes=scratch,
            compiler_params=pltpu.CompilerParams(
                collective_id=0, has_side_effects=True, vmem_limit_bytes=61 * 1024 * 1024
            ),
        )(*args[:3], *args[7:], *args[3:7])
        return tuple(v.transpose(0, 2, 1, 3).reshape(NX, NY, 2 * ZL) for v in made[:2]) + tuple(made[2:])

    return jax.shard_map(
        local,
        mesh=mesh,
        in_specs=(
            P("gx", "gy", None),
            P("gx", "gy", None),
            P(None, "gx", "gy", None),
            P(("gx", "gy")),
            P(("gx", "gy")),
            P("gx", "gy", None),
            P("gx", "gy", None),
            P("gx", "gy", None),
            P("gx", "gy", None),
        ),
        out_specs=(P("gx", "gy", None), P("gx", "gy", None), P(("gx", "gy")), P(("gx", "gy"))),
        check_vma=False,
    )
```
